128 devices in a mesh: sub: 8 (over x, core), beam: 8 (over y_hi, z), comp: 2 (over y_lo).
Axes of the slice: x: 4, y: 4 (y_hi: 2, y_lo: 2; y = y_hi * 2 + y_lo), z: 4, core: 2. Of those that a mesh axis runs over, the one named last changes fastest.
Arguments:
- raw_pulses: bfloat16 [16384, 2, 16384], P(('sub', 'beam', 'comp')), may hold values from -6 to 6
- range_filter: float32 [2, 16384], replicated, may hold values from -4 to 4
- steer_angle: float32 [128, 16384], P(None, ('sub', 'beam', 'comp')), may hold values from -3.140625 to 3.140625
- band_offsets: int32 [2, 1792], P(None, ('beam', 'comp')), may hold values from -4 to 28, as said below
- band_weights: float32 [2, 1792, 8], P(None, ('beam', 'comp')), may hold values from -1.5 to 1.5
- beam_delay: float32 [2, 1792], P(None, ('beam', 'comp')), may hold values from -3 to 3
Outputs:
- scene_beams: float32 [1024, 2, 16384], P(('beam', 'comp'), None, 'sub')
The draws below stay inside these ranges and needn't reach their ends.
Inputs may be any that keep to these rules, and one draw needn't show every extreme that they name: `band_offsets`: for new beam u of a merge level l and a block (0 <= u < 2 * 8 2^l), each side's offset is u // 2 - 8 // 2 + 1 or one less; the first beam of every level and block takes the lesser value, the last the greater.
All inputs are finite; a program needn't handle non-finite values.
Results may differ from the reference program's by a relative error of at most 0.0059.
Values may be sent and summed in bfloat16 or wider, within the bound.
No kernel may reach another device: no remote copies, remote signals or barrier semaphores. Data moves between devices by JAX's collectives and lax.ppermute only.
A program may use at most 128 MiB of HBM per device.

```python
import math
import jax
import jax.numpy as jnp
from jax import lax

NR = 16384
RADIX = 128
NB0 = 8
BAND = 8
PDEV = 128
PSUB = 2048
PULSES = 16384
NBT0 = 128
NEWL = 112
LEVELS = 3
N_SUB = 8
N_BEAM = 8
N_COMP = 2


def draw_band_offsets(key, part):
    blocks = N_BEAM * N_COMP
    centers = []
    first_flags = []
    last_flags = []
    for level_index in range(LEVELS):
        new_beams = 2 * NB0 * 2 ** level_index
        local_beam = jnp.arange(new_beams, dtype=jnp.int32)
        centers.append(local_beam // 2 - BAND // 2 + 1)
        first_flags.append(local_beam == 0)
        last_flags.append(local_beam == new_beams - 1)
    center_row = jnp.concatenate(centers)
    first_row = jnp.concatenate(first_flags)
    last_row = jnp.concatenate(last_flags)
    coin_flip = jax.random.randint(key, (2, blocks, NEWL), 0, 2, dtype=jnp.int32)
    lowered = jnp.where(first_row[None, None, :], 1, jnp.where(last_row[None, None, :], 0, coin_flip))
    return (center_row[None, None, :] - lowered).astype(jnp.int32).reshape(2, blocks * NEWL)


def levels(stream_key, shape, cuts, low, top_value):
    def one(axis_at, blocks):
        heights = jax.random.uniform(jax.random.fold_in(jax.random.fold_in(stream_key, 6), axis_at), (blocks,), jnp.float32, low / len(cuts), top_value / len(cuts))
        return jnp.repeat(jnp.exp(heights), shape[axis_at] // blocks).reshape((-1,) + (1,) * (len(shape) - axis_at - 1))

    loudness = one(*cuts[0])
    for cut in cuts[1:]:
        loudness = loudness * one(*cut)
    return loudness


def centred(key, dims, spread, bound, split=(), kind=jnp.bfloat16):
    drawn = jax.random.normal(key, dims, jnp.float32) * spread
    if len(split) > 0:
        drawn = levels(key, dims, split, -0.22, 0.18) * drawn
    return jnp.clip(drawn, min=-bound, max=bound).astype(kind)


def setup_inputs(seed: int = 0) -> dict:
    key_of = jax.random.split(jax.random.key(seed), 7)
    raw_pulses = centred(key_of[0], (PULSES, 2, NR), 1.0, 6.0, ((0, 128),))
    range_filter = centred(key_of[1], (2, NR), 0.7071, 4.0, (), jnp.float32)
    steer_angle = jnp.clip(jax.random.uniform(key_of[2], (NBT0, PULSES), jnp.float32, -3.140625, 3.140625), -3.140625, 3.140625)
    band_offsets = draw_band_offsets(jax.random.fold_in(key_of[6], 71), 0)
    band_weights = centred(key_of[4], (2, NEWL * N_BEAM * N_COMP, BAND), 0.25, 1.5, ((1, 16),), jnp.float32)
    beam_delay = jnp.clip(jax.random.uniform(key_of[5], (2, NEWL * N_BEAM * N_COMP), jnp.float32, -3.0, 3.0) * levels(key_of[5], (2, NEWL * N_BEAM * N_COMP), ((1, 16),), -0.4, 0.0), -3.0, 3.0)
    return dict(raw_pulses=raw_pulses, range_filter=range_filter, steer_angle=steer_angle, band_offsets=band_offsets, band_weights=band_weights, beam_delay=beam_delay)


def dft_table(length):
    index_row = jnp.arange(length, dtype=jnp.int32)
    product = (index_row[:, None] * index_row[None, :]) % length
    phase_angle = product.astype(jnp.float32) * (2.0 * math.pi / length)
    return jnp.cos(phase_angle).astype(jnp.bfloat16), (-jnp.sin(phase_angle)).astype(jnp.bfloat16)


def real_form(length):
    cos_part, sin_part = dft_table(length)
    upper_rows = jnp.concatenate([cos_part, sin_part], axis=1)
    lower_rows = jnp.concatenate([-sin_part, cos_part], axis=1)
    return jnp.concatenate([upper_rows, lower_rows], axis=0)


def twiddle():
    freq_index = jnp.arange(RADIX, dtype=jnp.int32)[:, None]
    time_index = jnp.arange(RADIX, dtype=jnp.int32)[None, :]
    phase_angle = ((freq_index * time_index) % NR).astype(jnp.float32) * (2.0 * math.pi / NR)
    return jnp.cos(phase_angle), -jnp.sin(phase_angle)


def compress(raw, range_filter):
    number = raw.shape[0]
    samples = raw.reshape(number, 2 * RADIX, RADIX).astype(jnp.float32)
    first_form = real_form(RADIX).astype(jnp.float32)
    section_one = jnp.einsum('pan,ak->pkn', samples, first_form, precision=lax.Precision.HIGHEST)
    cos_part, sin_part = twiddle()
    real_in = section_one[:, :RADIX]
    imag_in = section_one[:, RADIX:]
    turned = jnp.stack([real_in * cos_part - imag_in * sin_part, real_in * sin_part + imag_in * cos_part], 1)
    turned = turned.astype(jnp.bfloat16).astype(jnp.float32)
    second = real_form(RADIX).reshape(2, RADIX, 2, RADIX).astype(jnp.float32)
    spectrum = jnp.einsum('prkn,rnsm->psmk', turned, second, precision=lax.Precision.HIGHEST)
    spectrum = spectrum.reshape(number, 2, NR)
    factor = NR ** -0.5
    real_out = (spectrum[:, 0] * range_filter[0] - spectrum[:, 1] * range_filter[1]) * factor
    imag_out = (spectrum[:, 0] * range_filter[1] + spectrum[:, 1] * range_filter[0]) * factor
    return jnp.stack([real_out, imag_out], 1).astype(jnp.bfloat16)


def steering(phase_angle, factor):
    real_part = (jnp.cos(phase_angle) * factor).astype(jnp.bfloat16)
    imag_part = (jnp.sin(phase_angle) * factor).astype(jnp.bfloat16)
    return jnp.stack([jnp.stack([real_part, -imag_part], -1), jnp.stack([imag_part, real_part], -1)], 1)


def beam_term(weights, pulses):
    return jnp.einsum('kspq,pqr->ksr', weights.astype(jnp.float32), pulses.astype(jnp.float32),
                      precision=lax.Precision.HIGHEST)


def band_matrix(offset, weight, span):
    tap_index = offset[:, None] + BAND // 2 + jnp.arange(BAND, dtype=jnp.int32)[None, :]
    matches = tap_index[:, :, None] == jnp.arange(span, dtype=jnp.int32)[None, None, :]
    return jnp.sum(jnp.where(matches, weight[:, :, None], jnp.zeros_like(weight)[:, :, None]), axis=1)


def merge_level(subimage, level_index, band_offsets, band_weights, beam_delay):
    blocks = N_BEAM * N_COMP
    old_beams = NB0 * 2 ** level_index
    new_beams = 2 * old_beams
    column_base = NB0 * (2 ** (level_index + 1) - 2)
    margin = BAND // 2
    groups = subimage.shape[0] // 2
    padded = jnp.pad(subimage, ((0, 0), (margin, margin), (0, 0), (0, 0)))
    paired = padded.reshape(groups, 2, padded.shape[1], 2, NR)
    range_rows = jnp.arange(NR, dtype=jnp.int32).astype(jnp.float32)
    pieces = []
    for block in range(blocks):
        window = paired[:, :, block * old_beams: block * old_beams + old_beams + 2 * margin]
        col_start = block * NEWL + column_base
        real_sum = jnp.zeros((groups, new_beams, NR), jnp.float32)
        imag_sum = jnp.zeros((groups, new_beams, NR), jnp.float32)
        for parity in range(2):
            matrix = band_matrix(band_offsets[parity, col_start:col_start + new_beams],
                                 band_weights[parity, col_start:col_start + new_beams], old_beams + 2 * margin)
            blended = jnp.einsum('jw,gwsr->gjsr', matrix, window[:, parity], precision=lax.Precision.HIGHEST)
            phase_angle = beam_delay[parity, col_start:col_start + new_beams][:, None] * (1.0 + range_rows / NR)[None, :]
            cosine = jnp.cos(phase_angle)
            sine_part = jnp.sin(phase_angle)
            real_sum = real_sum + (cosine * blended[:, :, 0] - sine_part * blended[:, :, 1])
            imag_sum = imag_sum + (sine_part * blended[:, :, 0] + cosine * blended[:, :, 1])
        pieces.append(jnp.stack([real_sum, imag_sum], 2))
    return jnp.concatenate(pieces, 1)


def reference(raw_pulses, range_filter, steer_angle, band_offsets, band_weights, beam_delay):
    blocks = N_BEAM * N_COMP
    runs = raw_pulses.reshape(N_SUB, blocks, PDEV, 2, NR)
    angles = steer_angle.reshape(NBT0, N_SUB, blocks, PDEV).transpose(1, 2, 0, 3)
    factor = float(PSUB) ** -0.5

    def subaperture(sub_item):
        def add_run(summed, run_item):
            pulses = compress(run_item[0], range_filter)
            weights = steering(run_item[1], factor)
            return summed + beam_term(weights, pulses), None

        summed, _ = lax.scan(add_run, jnp.zeros((NBT0, 2, NR), jnp.float32), sub_item)
        return summed

    subimage = lax.map(subaperture, (runs, angles))
    for level_index in range(LEVELS):
        subimage = merge_level(subimage, level_index, band_offsets, band_weights, beam_delay)
    return subimage[0]
```

```python
import functools
import math

import jax
import jax.numpy as jnp
import ml_dtypes
import numpy as np
from jax import lax
from jax.experimental import pallas as pl
from jax.experimental.pallas import tpu as pltpu
from jax.sharding import Mesh
from jax.sharding import PartitionSpec as P

NR = 16384
RADIX = 128
NB0 = 8
BAND = 8
PSUB = 2048
RING = 4
HALF = NR // 2
TILE = 2048
SLAB = NR // 8
COLS = 512
SIDE = 208
BEAM_COMP = ("y_hi", "z", "y_lo")
SUB_BEAM_COMP = ("sub", "y_hi", "z", "y_lo")
Y = ("y_hi", "y_lo")
Z = "z"
BF = jnp.bfloat16
F4 = jnp.float32
ORDER = (
    (2, 0), (2, 1), (1, 2), (1, 3),
    (2, 2), (2, 3), (3, 0), (3, 1),
    (1, 0), (1, 1),
    (3, 2), (3, 3),
    (0, 0), (0, 1), (0, 2), (0, 3),
)
PARTS = (64, 64, 32, 32, 64)


def params(mebibytes):
    return pltpu.CompilerParams(vmem_limit_bytes=mebibytes << 20)


def real_form_transposed():
    index = np.arange(RADIX)
    angle = (index[:, None] * index[None, :] % RADIX) * (2.0 * math.pi / RADIX)
    cos_part, sin_part = np.cos(angle), -np.sin(angle)
    upper = np.concatenate([cos_part, sin_part], 1)
    lower = np.concatenate([-sin_part, cos_part], 1)
    return np.concatenate([upper, lower], 0).T.astype(ml_dtypes.bfloat16)


def twiddle():
    index = np.arange(RADIX)
    angle = (index[:, None] * index[None, :] % NR) * (2.0 * math.pi / NR)
    return np.stack([np.cos(angle), -np.sin(angle)]).astype(np.float32)


def ring_send(x, axis, step):
    return lax.ppermute(x, axis, [(k, (k + step) % RING) for k in range(RING)])


def beam_kernel(order_ref, angle_ref, raw_ref, *rest):
    outs, weights = rest[:-1], rest[-1]

    @pl.when(pl.program_id(0) == 0)
    def _():
        rows = lax.broadcasted_iota(jnp.int32, (128, 256), 0)
        cols = lax.broadcasted_iota(jnp.int32, (128, 256), 1)
        spread = jnp.where(cols // 2 == rows, 1.0, 0.0).astype(F4)
        angle = jnp.dot(
            angle_ref[...], spread, precision=lax.Precision.HIGHEST, preferred_element_type=F4
        )
        factor = float(PSUB) ** -0.5
        cosine = jnp.cos(angle) * factor
        sine = jnp.sin(angle) * factor
        even = cols % 2 == 0
        weights[0] = jnp.where(even, cosine, -sine)
        weights[1] = jnp.where(even, sine, cosine)

    picked = []
    for k in range(16):
        first = pl.multiple_of(order_ref[k] * NB0, NB0)
        picked.append(weights[0, pl.ds(first, NB0), :])
        picked.append(weights[1, pl.ds(first, NB0), :])
    matrix = jnp.concatenate(picked, 0).astype(BF)
    raw = raw_ref[...].reshape(256, raw_ref.shape[2])
    total = jnp.dot(matrix, raw, preferred_element_type=F4).astype(BF)
    start = 0
    for out in outs:
        size = out.shape[0]
        out[...] = total[start : start + size]
        start += size


def beam_sums(order, angles, raw, half):
    steps = HALF // TILE
    return pl.pallas_call(
        beam_kernel,
        grid_spec=pltpu.PrefetchScalarGridSpec(
            num_scalar_prefetch=1,
            grid=(steps,),
            in_specs=[
                pl.BlockSpec((128, 128), lambda i, o: (0, 0)),
                pl.BlockSpec((128, 2, TILE), lambda i, o: (0, 0, i + half * steps)),
            ],
            out_specs=[pl.BlockSpec((n, TILE), lambda i, o: (0, i)) for n in PARTS],
            scratch_shapes=[pltpu.VMEM((2, 128, 256), F4)],
        ),
        out_shape=[jax.ShapeDtypeStruct((n, HALF), BF) for n in PARTS],
        compiler_params=params(40),
        name="beam_sums",
    )(order, angles, raw)


def relay_kernel(q1, q3, p1, m1, s, t):
    s[...] = (q1[...].astype(F4) + p1[...].astype(F4)).astype(BF)
    t[...] = (q3[...].astype(F4) + m1[...].astype(F4)).astype(BF)


def relay_sums(q1, q3, p1, m1, tile):
    rows, cols = q1.shape
    spec = pl.BlockSpec((rows, tile), lambda i: (0, i))
    return pl.pallas_call(
        relay_kernel,
        grid=(cols // tile,),
        in_specs=[spec] * 4,
        out_specs=[spec] * 2,
        out_shape=[jax.ShapeDtypeStruct((rows, cols), BF)] * 2,
        name="relay_sums",
    )(q1, q3, p1, m1)


def middle_kernel(own, p1, m1, p2, m2, plus, minus, q1, q3, keep):
    low = own[:32].astype(F4) + m1[...].astype(F4) + p2[...].astype(F4)
    high = own[32:].astype(F4) + p1[...].astype(F4) + m2[...].astype(F4)
    keep[...] = low[:16]
    q1[...] = low[16:24].astype(BF)
    plus[...] = jnp.concatenate([high[:8], low[24:]], 0).astype(BF)
    minus[...] = jnp.concatenate([high[8:16], high[16:24]], 0).astype(BF)
    q3[...] = high[24:].astype(BF)


def middle_sums(own, p1, m1, p2, m2):
    tile = 2048
    outs = ((16, BF), (16, BF), (8, BF), (8, BF), (16, F4))
    received = pl.BlockSpec((32, tile), lambda i: (1, i))
    return pl.pallas_call(
        middle_kernel,
        grid=(HALF // tile,),
        in_specs=[pl.BlockSpec((64, tile), lambda i: (0, i)), received, received]
        + [pl.BlockSpec((32, tile), lambda i: (0, i))] * 2,
        out_specs=[pl.BlockSpec((n, tile), lambda i: (0, i)) for n, _ in outs],
        out_shape=[jax.ShapeDtypeStruct((n, HALF), d) for n, d in outs],
        name="middle_sums",
    )(own, p1, m1, p2, m2)


def compress_kernel(*refs):
    ins, (form_ref, turn_ref, filter_ref, out, lines, bins) = refs[:10], refs[10:]
    for half in range(2):
        keep, p3, m3, p4, m4 = ins[5 * half : 5 * half + 5]
        sums = (
            keep[:8] + m3[...].astype(F4)[8:] + p4[...].astype(F4),
            keep[8:] + p3[...].astype(F4)[8:] + m4[...].astype(F4),
        )
        for part in range(2):
            for k in range(64):
                row = (half * 64 + k) * 8
                lines[part, row : row + 8, :] = sums[part][:, k * 128 : (k + 1) * 128]
    form = form_ref[...]
    cos_part, sin_part = turn_ref[0], turn_ref[1]
    scale = NR ** (-0.5)
    real_filter, imag_filter = filter_ref[0] * scale, filter_ref[1] * scale
    for beam in range(NB0):
        picked = pl.ds(beam, 128, stride=8)
        data = jnp.concatenate([lines[0, picked, :], lines[1, picked, :]], 0)
        upper = data.astype(BF)
        lower = (data - upper.astype(F4)).astype(BF)
        one = jnp.dot(form, jnp.concatenate([upper, lower], 1), preferred_element_type=F4)
        one = one[:, :128] + one[:, 128:]
        real_in, imag_in = one[:128], one[128:]
        turned = jnp.concatenate(
            [real_in * cos_part - imag_in * sin_part, real_in * sin_part + imag_in * cos_part], 1
        )
        upper = turned.astype(BF)
        lower = (turned - upper.astype(F4)).astype(BF)
        two = lax.dot_general(
            form,
            jnp.concatenate([upper, lower], 0),
            (((1,), (1,)), ((), ())),
            preferred_element_type=F4,
        )
        two = two[:, :128] + two[:, 128:]
        real_in, imag_in = two[:128], two[128:]
        bins[0, picked, :] = real_in * real_filter - imag_in * imag_filter
        bins[1, picked, :] = real_in * imag_filter + imag_in * real_filter
    for slab in range(8):
        for k in range(16):
            row = (slab * 16 + k) * 8
            both = jnp.concatenate([bins[0, row : row + 8, :], bins[1, row : row + 8, :]], 0)
            out[slab, :, k * 128 : (k + 1) * 128] = both.astype(BF)


def compressed_beams(pieces, range_filter):
    return pl.pallas_call(
        compress_kernel,
        out_shape=jax.ShapeDtypeStruct((8, 16, SLAB), BF),
        scratch_shapes=[pltpu.VMEM((2, 1024, 128), F4), pltpu.VMEM((2, 1024, 128), F4)],
        compiler_params=params(40),
        name="compressed_beams",
    )(
        *pieces,
        jnp.asarray(real_form_transposed()),
        jnp.asarray(twiddle()),
        range_filter.reshape(2, 128, 128),
    )


def table_kernel(start_ref, table_ref, matrix, near_a, near_b, far_cos, far_sin):
    rows = table_ref.shape[0]
    lane = lax.broadcasted_iota(jnp.int32, (rows, 128), 1)
    row = lax.broadcasted_iota(jnp.int32, (rows, 128), 0) % SIDE
    lane_f = lane.astype(F4)
    table = table_ref[...]
    offset = table[:, 0:1]
    total = jnp.zeros((rows, 128), F4)
    for tap in range(BAND):
        total = total + jnp.where(lane_f == offset + float(tap), table[:, tap + 1 : tap + 2], 0.0)
    matrix[...] = total
    delay = table[:, 9:10]
    step = delay * (lane_f * (1.0 / NR))
    far_cos[...] = jnp.cos(step)
    far_sin[...] = jnp.sin(step)
    first = start_ref[0].astype(F4)
    base = delay * (1.0 + (first + lane_f * 128.0) * (1.0 / NR))
    cosine, sine = jnp.cos(base), jnp.sin(base)
    odd = (row >= 80) & (row % 2 == 1)
    value_a = jnp.where(odd, sine, cosine)
    value_b = jnp.where(odd, cosine, -sine)
    for tile in range(SLAB // COLS):
        lanes = slice(tile * 4, tile * 4 + 4)
        near_a[tile, :, 0:4] = value_a[:, lanes]
        near_b[tile, :, 0:4] = value_b[:, lanes]


def merge_tables(start, table):
    rows = table.shape[0]
    tiles = SLAB // COLS
    one = jax.ShapeDtypeStruct((rows, 128), F4)
    many = jax.ShapeDtypeStruct((tiles, rows, 128), F4)
    vmem = pl.BlockSpec(memory_space=pltpu.VMEM)
    return pl.pallas_call(
        table_kernel,
        in_specs=[pl.BlockSpec(memory_space=pltpu.SMEM), vmem],
        out_specs=[vmem] * 5,
        out_shape=[one, many, many, one, one],
        compiler_params=params(40),
        name="merge_tables",
    )(start, table)


def split_rows(matrix):
    upper = matrix.astype(BF)
    return upper, (matrix - upper.astype(F4)).astype(BF)


def merge_kernel(left, own, right, matrix, near_a, near_b, far_cos, far_sin, out):
    dot = functools.partial(jnp.dot, preferred_element_type=F4)

    def phases(first, count):
        rows = slice(first, first + count)
        cosine, sine = far_cos[rows, :], far_sin[rows, :]
        real_parts, imag_parts = [], []
        for k in range(COLS // 128):
            a, b = near_a[0, rows, k : k + 1], near_b[0, rows, k : k + 1]
            real_parts.append(a * cosine + b * sine)
            imag_parts.append(b * cosine - a * sine)
        return jnp.concatenate(real_parts, 1), jnp.concatenate(imag_parts, 1)

    def blend(matrices, image, exact):
        upper, lower = matrices
        rows = upper.shape[0]
        if exact:
            both = dot(jnp.concatenate([upper, lower], 0), image.astype(BF))
            return both[:rows] + both[rows:]
        high = image.astype(BF)
        low = (image - high.astype(F4)).astype(BF)
        both = dot(jnp.concatenate([upper, lower], 0), high)
        return both[:rows] + both[rows:] + dot(upper, low)

    zeros = jnp.zeros((8, COLS), F4)
    images = []
    for side in range(8):
        parts = [ref[side].astype(F4) for ref in (left, own, right)]
        images.append(
            tuple(jnp.concatenate([p[8 * q : 8 * q + 8] for p in parts] + [zeros], 0) for q in (0, 1))
        )
    for first, count, depth in ((0, 32, 32), (32, 48, 32)):
        sides = [
            (
                split_rows(matrix[c * SIDE + first : c * SIDE + first + count, :depth]),
                phases(c * SIDE + first, count),
            )
            for c in range(2)
        ]
        merged = []
        for group in range(len(images) // 2):
            real_sum, imag_sum = None, None
            for c, (matrices, (a, b)) in enumerate(sides):
                real_in, imag_in = (
                    blend(matrices, images[2 * group + c][q], first == 0) for q in (0, 1)
                )
                real_out = a * real_in + b * imag_in
                imag_out = a * imag_in - b * real_in
                real_sum = real_out if c == 0 else real_sum + real_out
                imag_sum = imag_out if c == 0 else imag_sum + imag_out
            merged.append((real_sum, imag_sum))
        images = merged
    total = None
    for c in range(2):
        rows = slice(c * SIDE + 80, c * SIDE + SIDE)
        matrices = split_rows(matrix[rows, :48])
        a, b = phases(c * SIDE + 80, 128)
        value = a * blend(matrices, images[c][0], False) + b * blend(matrices, images[c][1], False)
        total = value if c == 0 else total + value
    out[...] = total.reshape(64, 2, COLS)


def merge(left, own, right, tables):
    matrix, near_a, near_b, far_cos, far_sin = tables
    rows = matrix.shape[0]
    image = pl.BlockSpec((8, 16, COLS), lambda i: (0, 0, i))
    whole = pl.BlockSpec((rows, 128), lambda i: (0, 0))
    tiled = pl.BlockSpec((1, rows, 128), lambda i: (i, 0, 0))
    return pl.pallas_call(
        merge_kernel,
        grid=(SLAB // COLS,),
        in_specs=[image] * 3 + [whole, tiled, tiled, whole, whole],
        out_specs=pl.BlockSpec((64, 2, COLS), lambda i: (0, 0, i)),
        out_shape=jax.ShapeDtypeStruct((64, 2, SLAB), F4),
        compiler_params=params(48),
        name="merge",
    )(left, own, right, matrix, near_a, near_b, far_cos, far_sin)


def from_neighbours(array):
    blocks = lax.axis_size(BEAM_COMP)
    left = lax.ppermute(array, BEAM_COMP, [(k, k + 1) for k in range(blocks - 1)])
    right = lax.ppermute(array, BEAM_COMP, [(k + 1, k) for k in range(blocks - 1)])
    return left, right


def band_table(band_offsets, band_weights, beam_delay):
    own = jnp.concatenate(
        [band_offsets.astype(F4)[:, :, None], band_weights, beam_delay[:, :, None]], 2
    )
    left, right = from_neighbours(own)
    pieces = [left[:, 8:16], own[:, 0:16], right[:, 0:8]]
    pieces += [left[:, 40:48], own[:, 16:48], right[:, 16:24]]
    pieces += [jnp.repeat(own[:, 48:112], 2, axis=1)]
    base = np.zeros((1, SIDE, 10), np.float32)
    spans = ((8, 0), (16, 8), (8, 16), (8, -8), (32, 8), (8, 24), (128, 8))
    base[0, :, 0] = np.concatenate([np.full(n, v) for n, v in spans])
    return (jnp.concatenate(pieces, 1) + base).reshape(2 * SIDE, 10)


def ring_half(order, angles, raw, half, first, second):
    plus, minus, q1, q3, own = beam_sums(order, angles, raw, half)
    p1 = ring_send(plus, first, 1)
    m1 = ring_send(minus, first, -1)
    s, t = relay_sums(q1, q3, p1, m1, 2048)
    p2 = ring_send(s, first, 1)
    m2 = ring_send(t, first, -1)
    plus, minus, q1, q3, keep = middle_sums(own, p1, m1, p2, m2)
    p3 = ring_send(plus, second, 1)
    m3 = ring_send(minus, second, -1)
    s, t = relay_sums(q1, q3, p3, m3, 8192)
    p4 = ring_send(s, second, 1)
    m4 = ring_send(t, second, -1)
    return keep, p3, m3, p4, m4


def body(raw_pulses, range_filter, steer_angle, band_offsets, band_weights, beam_delay):
    y_index = lax.axis_index(Y)
    z_index = lax.axis_index(Z)
    near = np.array(ORDER, np.int32)

    def block_of(y, z):
        y, z = y % RING, z % RING
        return (y // 2) * 8 + z * 2 + y % 2

    order_z = block_of(y_index + near[:, 1], z_index + near[:, 0]).astype(jnp.int32)
    order_y = block_of(y_index + near[:, 0], z_index + near[:, 1]).astype(jnp.int32)
    pieces = ring_half(order_z, steer_angle, raw_pulses, 0, Z, Y)
    pieces += ring_half(order_y, steer_angle, raw_pulses, 1, Y, Z)
    table = band_table(band_offsets, band_weights, beam_delay)
    start = (lax.axis_index("sub") * SLAB).astype(jnp.int32).reshape(1)
    tables = merge_tables(start, table)
    beams = compressed_beams(pieces, range_filter)
    image = lax.all_to_all(beams, "sub", 0, 0, tiled=True)
    left, right = from_neighbours(image)
    return merge(left, image, right, tables)


def solution(mesh):
    split = Mesh(
        mesh.devices.reshape(mesh.shape["sub"], 2, RING, mesh.shape["comp"]), SUB_BEAM_COMP
    )
    return jax.shard_map(
        body,
        mesh=split,
        in_specs=(
            P(SUB_BEAM_COMP, None, None),
            P(),
            P(None, SUB_BEAM_COMP),
            P(None, BEAM_COMP),
            P(None, BEAM_COMP, None),
            P(None, BEAM_COMP),
        ),
        out_specs=P(BEAM_COMP, None, "sub"),
        check_vma=False,
    )
```

```python
import functools
import math

import jax
import jax.numpy as jnp
import ml_dtypes
import numpy as np
from jax import lax
from jax.experimental import pallas as pl
from jax.experimental.pallas import tpu as pltpu
from jax.sharding import Mesh
from jax.sharding import PartitionSpec as P

NR = 16384
RADIX = 128
NB0 = 8
BAND = 8
PSUB = 2048
RING = 4
HALF = NR // 2
TILE = 2048
SLAB = NR // 8
COLS = 512
SIDE = 208
BEAM_COMP = ("y_hi", "z", "y_lo")
SUB_BEAM_COMP = ("sub", "y_hi", "z", "y_lo")
Y = ("y_hi", "y_lo")
Z = "z"
BF = jnp.bfloat16
F4 = jnp.float32
SENT = ((2, 0), (2, 1), (1, 2), (1, 3), (2, 2), (2, 3), (3, 0), (3, 1))
KEPT = ((1, 0), (1, 1), (3, 2), (3, 3), (0, 0), (0, 1), (0, 2), (0, 3))
SENT_ROWS = (64, 64)
KEPT_ROWS = (32, 32, 64)


def params(mebibytes):
    return pltpu.CompilerParams(vmem_limit_bytes=mebibytes << 20)


def real_form_transposed():
    index = np.arange(RADIX)
    angle = (index[:, None] * index[None, :] % RADIX) * (2.0 * math.pi / RADIX)
    cos_part, sin_part = np.cos(angle), -np.sin(angle)
    upper = np.concatenate([cos_part, sin_part], 1)
    lower = np.concatenate([-sin_part, cos_part], 1)
    return np.concatenate([upper, lower], 0).T.astype(ml_dtypes.bfloat16)


def twiddle():
    index = np.arange(RADIX)
    angle = (index[:, None] * index[None, :] % NR) * (2.0 * math.pi / NR)
    return np.stack([np.cos(angle), -np.sin(angle)]).astype(np.float32)


def ring_send(x, axis, step):
    return lax.ppermute(x, axis, [(k, (k + step) % RING) for k in range(RING)])


def steering_rows(angle_ref, weights):
    factor = float(PSUB) ** -0.5
    rows = lax.broadcasted_iota(jnp.int32, (128, 256), 0)
    cols = lax.broadcasted_iota(jnp.int32, (128, 256), 1)
    spread = jnp.where(cols // 2 == rows, 1.0, 0.0).astype(BF)
    angle = angle_ref[...]
    cosine = (jnp.cos(angle) * factor).astype(BF)
    sine = (jnp.sin(angle) * factor).astype(BF)
    cosine = jnp.dot(cosine, spread, preferred_element_type=F4)
    sine = jnp.dot(sine, spread, preferred_element_type=F4)
    even = cols % 2 == 0
    weights[0] = jnp.where(even, cosine, -sine)
    weights[1] = jnp.where(even, sine, cosine)


def beam_products(weights, raw_ref, owners, z_first, outs):
    y = lax.axis_index("y_hi") * 2 + lax.axis_index("y_lo")
    z = lax.axis_index("z")
    picked = []
    for first, second in owners:
        y_step, z_step = (second, first) if z_first else (first, second)
        y_of, z_of = lax.rem(y + y_step, RING), lax.rem(z + z_step, RING)
        block = lax.div(y_of, 2) * 8 + z_of * 2 + lax.rem(y_of, 2)
        start = pl.multiple_of(block * NB0, NB0)
        picked.append(weights[0, pl.ds(start, NB0), :])
        picked.append(weights[1, pl.ds(start, NB0), :])
    matrix = jnp.concatenate(picked, 0).astype(BF)
    raw = raw_ref[...].reshape(256, raw_ref.shape[2])
    total = jnp.dot(matrix, raw, preferred_element_type=F4).astype(BF)
    start = 0
    for out in outs:
        size = out.shape[0]
        out[...] = total[start : start + size]
        start += size


def opening_kernel(angle_ref, raw_ref, plus, minus, weights):
    @pl.when(pl.program_id(0) == 0)
    def _():
        steering_rows(angle_ref, weights)

    beam_products(weights, raw_ref, SENT, True, (plus, minus))


def later_kernel(owners, z_first, weights, raw_ref, *outs):
    beam_products(weights, raw_ref, owners, z_first, outs)


def beam_sums(kernel, small, raw, half, sizes, with_weights):
    steps = HALF // TILE
    weights = (2, 128, 256)

    def fixed(shape):
        return pl.BlockSpec(shape, lambda i: (0,) * len(shape))

    return pl.pallas_call(
        kernel,
        grid=(steps,),
        in_specs=[
            fixed(small.shape),
            pl.BlockSpec((128, 2, TILE), lambda i: (0, 0, i + half * steps)),
        ],
        out_specs=[pl.BlockSpec((n, TILE), lambda i: (0, i)) for n in sizes]
        + [fixed(weights)] * with_weights,
        out_shape=[pltpu.HBM((n, HALF), BF) for n in sizes]
        + [jax.ShapeDtypeStruct(weights, F4)] * with_weights,
        compiler_params=params(16),
        name="beam_sums",
    )(small, pltpu.with_memory_space_constraint(raw, pltpu.HBM))


def relay(q, received):
    rows = q.shape[0]
    return (q.astype(F4) + received[:rows].astype(F4)).astype(BF)


def middle_kernel(own, p1, m1, p2, m2, plus, minus, q1, q3, keep):
    tile = 512

    def step(k, carry):
        cols = pl.ds(pl.multiple_of(k * tile, tile), tile)
        low = own[:32, cols].astype(F4) + m1[32:, cols].astype(F4) + p2[:, cols].astype(F4)
        high = own[32:, cols].astype(F4) + p1[32:, cols].astype(F4) + m2[:, cols].astype(F4)
        keep[:, cols] = low[:16]
        q1[:, cols] = low[16:24].astype(BF)
        plus[:, cols] = jnp.concatenate([high[:8], low[24:]], 0).astype(BF)
        minus[:, cols] = jnp.concatenate([high[8:16], high[16:24]], 0).astype(BF)
        q3[:, cols] = high[24:].astype(BF)
        return carry

    lax.fori_loop(0, HALF // tile, step, 0)


def middle_sums(own, p1, m1, p2, m2):
    outs = ((16, BF), (16, BF), (8, BF), (8, BF), (16, F4))
    vmem = pl.BlockSpec(memory_space=pltpu.VMEM)
    return pl.pallas_call(
        middle_kernel,
        in_specs=[vmem] * 5,
        out_specs=[vmem] * 5,
        out_shape=[jax.ShapeDtypeStruct((n, HALF), d) for n, d in outs],
        compiler_params=params(4),
        name="middle_sums",
    )(own, p1, m1, p2, m2)


def compress_kernel(*refs):
    ins, (form_ref, turn_ref, filter_ref, out, lines, bins) = refs[:10], refs[10:]
    for half in range(2):
        keep, p3, m3, p4, m4 = ins[5 * half : 5 * half + 5]
        sums = (
            keep[:8] + m3[...].astype(F4)[8:] + p4[...].astype(F4),
            keep[8:] + p3[...].astype(F4)[8:] + m4[...].astype(F4),
        )
        for part in range(2):
            for k in range(64):
                row = (half * 64 + k) * 8
                lines[part, row : row + 8, :] = sums[part][:, k * 128 : (k + 1) * 128]
    form = form_ref[...]
    cos_part, sin_part = turn_ref[0], turn_ref[1]
    scale = NR ** (-0.5)
    real_filter, imag_filter = filter_ref[0] * scale, filter_ref[1] * scale
    for beam in range(NB0):
        picked = pl.ds(beam, 128, stride=8)
        data = jnp.concatenate([lines[0, picked, :], lines[1, picked, :]], 0)
        upper = data.astype(BF)
        lower = (data - upper.astype(F4)).astype(BF)
        one = jnp.dot(form, jnp.concatenate([upper, lower], 1), preferred_element_type=F4)
        one = one[:, :128] + one[:, 128:]
        real_in, imag_in = one[:128], one[128:]
        turned = jnp.concatenate(
            [real_in * cos_part - imag_in * sin_part, real_in * sin_part + imag_in * cos_part], 1
        )
        upper = turned.astype(BF)
        lower = (turned - upper.astype(F4)).astype(BF)
        two = lax.dot_general(
            form,
            jnp.concatenate([upper, lower], 0),
            (((1,), (1,)), ((), ())),
            preferred_element_type=F4,
        )
        two = two[:, :128] + two[:, 128:]
        real_in, imag_in = two[:128], two[128:]
        bins[0, picked, :] = real_in * real_filter - imag_in * imag_filter
        bins[1, picked, :] = real_in * imag_filter + imag_in * real_filter
    for slab in range(8):
        for k in range(16):
            row = (slab * 16 + k) * 8
            both = jnp.concatenate([bins[0, row : row + 8, :], bins[1, row : row + 8, :]], 0)
            out[slab, :, k * 128 : (k + 1) * 128] = both.astype(BF)


def compressed_beams(pieces, range_filter):
    return pl.pallas_call(
        compress_kernel,
        out_shape=jax.ShapeDtypeStruct((8, 16, SLAB), BF),
        scratch_shapes=[pltpu.VMEM((2, 1024, 128), F4), pltpu.VMEM((2, 1024, 128), F4)],
        compiler_params=params(12),
        name="compressed_beams",
    )(
        *pieces,
        jnp.asarray(real_form_transposed()),
        jnp.asarray(twiddle()),
        range_filter.reshape(2, 128, 128),
    )


def table_kernel(start_ref, table_ref, matrix, near_a, near_b, far_cos, far_sin):
    rows = table_ref.shape[0]
    lane = lax.broadcasted_iota(jnp.int32, (rows, 128), 1)
    row = lax.broadcasted_iota(jnp.int32, (rows, 128), 0) % SIDE
    lane_f = lane.astype(F4)
    table = table_ref[...]
    offset = table[:, 0:1]
    total = jnp.zeros((rows, 128), F4)
    for tap in range(BAND):
        total = total + jnp.where(lane_f == offset + float(tap), table[:, tap + 1 : tap + 2], 0.0)
    matrix[...] = total
    delay = table[:, 9:10]
    step = delay * (lane_f * (1.0 / NR))
    far_cos[...] = jnp.cos(step)
    far_sin[...] = jnp.sin(step)
    first = start_ref[0].astype(F4)
    base = delay * (1.0 + (first + lane_f * 128.0) * (1.0 / NR))
    cosine, sine = jnp.cos(base), jnp.sin(base)
    odd = (row >= 80) & (row % 2 == 1)
    value_a = jnp.where(odd, sine, cosine)
    value_b = jnp.where(odd, cosine, -sine)
    for tile in range(SLAB // COLS):
        lanes = slice(tile * 4, tile * 4 + 4)
        near_a[tile, :, 0:4] = value_a[:, lanes]
        near_b[tile, :, 0:4] = value_b[:, lanes]


def merge_tables(start, table):
    rows = table.shape[0]
    tiles = SLAB // COLS
    one = jax.ShapeDtypeStruct((rows, 128), F4)
    many = jax.ShapeDtypeStruct((tiles, rows, 128), F4)
    vmem = pl.BlockSpec(memory_space=pltpu.VMEM)
    return pl.pallas_call(
        table_kernel,
        in_specs=[pl.BlockSpec(memory_space=pltpu.SMEM), vmem],
        out_specs=[vmem] * 5,
        out_shape=[one, many, many, one, one],
        compiler_params=params(12),
        name="merge_tables",
    )(start, table)


def split_rows(matrix):
    upper = matrix.astype(BF)
    return upper, (matrix - upper.astype(F4)).astype(BF)


def merge_kernel(left, own, right, matrix, near_a, near_b, far_cos, far_sin, out):
    dot = functools.partial(jnp.dot, preferred_element_type=F4)

    def phases(first, count):
        rows = slice(first, first + count)
        cosine, sine = far_cos[rows, :], far_sin[rows, :]
        real_parts, imag_parts = [], []
        for k in range(COLS // 128):
            a, b = near_a[0, rows, k : k + 1], near_b[0, rows, k : k + 1]
            real_parts.append(a * cosine + b * sine)
            imag_parts.append(b * cosine - a * sine)
        return jnp.concatenate(real_parts, 1), jnp.concatenate(imag_parts, 1)

    def blend(matrices, image, exact):
        upper, lower = matrices
        rows = upper.shape[0]
        if exact:
            both = dot(jnp.concatenate([upper, lower], 0), image.astype(BF))
            return both[:rows] + both[rows:]
        high = image.astype(BF)
        low = (image - high.astype(F4)).astype(BF)
        both = dot(jnp.concatenate([upper, lower], 0), high)
        return both[:rows] + both[rows:] + dot(upper, low)

    zeros = jnp.zeros((8, COLS), F4)
    images = []
    for side in range(8):
        parts = [ref[side].astype(F4) for ref in (left, own, right)]
        images.append(
            tuple(jnp.concatenate([p[8 * q : 8 * q + 8] for p in parts] + [zeros], 0) for q in (0, 1))
        )
    for first, count, depth in ((0, 32, 32), (32, 48, 32)):
        sides = [
            (
                split_rows(matrix[c * SIDE + first : c * SIDE + first + count, :depth]),
                phases(c * SIDE + first, count),
            )
            for c in range(2)
        ]
        merged = []
        for group in range(len(images) // 2):
            real_sum, imag_sum = None, None
            for c, (matrices, (a, b)) in enumerate(sides):
                real_in, imag_in = (
                    blend(matrices, images[2 * group + c][q], first == 0) for q in (0, 1)
                )
                real_out = a * real_in + b * imag_in
                imag_out = a * imag_in - b * real_in
                real_sum = real_out if c == 0 else real_sum + real_out
                imag_sum = imag_out if c == 0 else imag_sum + imag_out
            merged.append((real_sum, imag_sum))
        images = merged
    total = None
    for c in range(2):
        rows = slice(c * SIDE + 80, c * SIDE + SIDE)
        matrices = split_rows(matrix[rows, :48])
        a, b = phases(c * SIDE + 80, 128)
        value = a * blend(matrices, images[c][0], False) + b * blend(matrices, images[c][1], False)
        total = value if c == 0 else total + value
    out[...] = total.reshape(64, 2, COLS)


def merge(left, own, right, tables):
    matrix, near_a, near_b, far_cos, far_sin = tables
    rows = matrix.shape[0]
    image = pl.BlockSpec((8, 16, COLS), lambda i: (0, 0, i))
    whole = pl.BlockSpec((rows, 128), lambda i: (0, 0))
    tiled = pl.BlockSpec((1, rows, 128), lambda i: (i, 0, 0))
    return pl.pallas_call(
        merge_kernel,
        grid=(SLAB // COLS,),
        in_specs=[image] * 3 + [whole, tiled, tiled, whole, whole],
        out_specs=pl.BlockSpec((64, 2, COLS), lambda i: (0, 0, i)),
        out_shape=jax.ShapeDtypeStruct((64, 2, SLAB), F4),
        compiler_params=params(24),
        name="merge",
    )(left, own, right, matrix, near_a, near_b, far_cos, far_sin)


def from_neighbours(array):
    blocks = lax.axis_size(BEAM_COMP)
    left = lax.ppermute(array, BEAM_COMP, [(k, k + 1) for k in range(blocks - 1)])
    right = lax.ppermute(array, BEAM_COMP, [(k + 1, k) for k in range(blocks - 1)])
    return left, right


def own_table(band_offsets, band_weights, beam_delay):
    return jnp.concatenate(
        [band_offsets.astype(F4)[:, :, None], band_weights, beam_delay[:, :, None]], 2
    )


def band_table(own):
    left, right = from_neighbours(own)
    pieces = [left[:, 8:16], own[:, 0:16], right[:, 0:8]]
    pieces += [left[:, 40:48], own[:, 16:48], right[:, 16:24]]
    pieces += [jnp.repeat(own[:, 48:112], 2, axis=1)]
    base = np.zeros((1, SIDE, 10), np.float32)
    spans = ((8, 0), (16, 8), (8, 16), (8, -8), (32, 8), (8, 24), (128, 8))
    base[0, :, 0] = np.concatenate([np.full(n, v) for n, v in spans])
    return (jnp.concatenate(pieces, 1) + base).reshape(2 * SIDE, 10)


def ring_start(parts, first):
    return ring_send(parts[0], first, 1), ring_send(parts[1], first, -1)


def ring_rest(kept, received, first, second):
    q1, q3, own = kept
    p1, m1 = received
    p2 = ring_send(relay(q1, p1), first, 1)
    m2 = ring_send(relay(q3, m1), first, -1)
    plus, minus, q1, q3, keep = middle_sums(own, p1, m1, p2, m2)
    p3 = ring_send(plus, second, 1)
    m3 = ring_send(minus, second, -1)
    p4 = ring_send(relay(q1, p3), second, 1)
    m4 = ring_send(relay(q3, m3), second, -1)
    return keep, p3, m3, p4, m4


def body(raw_pulses, range_filter, steer_angle, band_offsets, band_weights, beam_delay):
    later = functools.partial
    angles = pltpu.with_memory_space_constraint(steer_angle, pltpu.HBM)
    *sent_z, weights = beam_sums(opening_kernel, angles, raw_pulses, 0, SENT_ROWS, True)
    received_z = ring_start(sent_z, Z)
    sent_y = beam_sums(later(later_kernel, SENT, False), weights, raw_pulses, 1, SENT_ROWS, False)
    received_y = ring_start(sent_y, Y)
    kept_z = beam_sums(later(later_kernel, KEPT, True), weights, raw_pulses, 0, KEPT_ROWS, False)
    kept_y = beam_sums(later(later_kernel, KEPT, False), weights, raw_pulses, 1, KEPT_ROWS, False)
    start = (lax.axis_index("sub") * SLAB).astype(jnp.int32).reshape(1)
    tables = merge_tables(start, band_table(own_table(band_offsets, band_weights, beam_delay)))
    pieces = ring_rest(kept_z, received_z, Z, Y)
    pieces += ring_rest(kept_y, received_y, Y, Z)
    beams = compressed_beams(pieces, range_filter)
    image = lax.all_to_all(beams, "sub", 0, 0, tiled=True)
    left, right = from_neighbours(image)
    return merge(left, image, right, tables)


def solution(mesh):
    split = Mesh(
        mesh.devices.reshape(mesh.shape["sub"], 2, RING, mesh.shape["comp"]), SUB_BEAM_COMP
    )
    return jax.shard_map(
        body,
        mesh=split,
        in_specs=(
            P(SUB_BEAM_COMP, None, None),
            P(),
            P(None, SUB_BEAM_COMP),
            P(None, BEAM_COMP),
            P(None, BEAM_COMP, None),
            P(None, BEAM_COMP),
        ),
        out_specs=P(BEAM_COMP, None, "sub"),
        check_vma=False,
    )
```

```python
import functools
import math

import jax
import jax.numpy as jnp
import ml_dtypes
import numpy as np
from jax import lax
from jax.experimental import pallas as pl
from jax.experimental.pallas import tpu as pltpu
from jax.sharding import Mesh
from jax.sharding import PartitionSpec as P

NR = 16384
RADIX = 128
NB0 = 8
BAND = 8
PSUB = 2048
RING = 4
HALF = NR // 2
READS = 4
READ = NR // READS
STEP = 2048
SLAB = NR // 8
COLS = 512
PIECES = 2
PIECE = SLAB // PIECES
DIRECT = (True, True)
SIDE = 208
BEAM_COMP = ("y_hi", "z", "y_lo")
SUB_BEAM_COMP = ("sub", "y_hi", "z", "y_lo")
Y = ("y_hi", "y_lo")
Z = "z"
BF = jnp.bfloat16
F4 = jnp.float32
SENT = ((2, 0), (2, 1), (1, 2), (1, 3), (2, 2), (2, 3), (3, 0), (3, 1))
KEPT = ((1, 0), (1, 1), (3, 2), (3, 3), (0, 0), (0, 1), (0, 2), (0, 3))
SENT_ROWS = (64, 64)
KEPT_ROWS = (32, 32, 64)


def params(mebibytes):
    return pltpu.CompilerParams(vmem_limit_bytes=mebibytes << 20)


def real_form_transposed():
    index = np.arange(RADIX)
    angle = (index[:, None] * index[None, :] % RADIX) * (2.0 * math.pi / RADIX)
    cos_part, sin_part = np.cos(angle), -np.sin(angle)
    upper = np.concatenate([cos_part, sin_part], 1)
    lower = np.concatenate([-sin_part, cos_part], 1)
    return np.concatenate([upper, lower], 0).T.astype(ml_dtypes.bfloat16)


def twiddle():
    index = np.arange(RADIX)
    angle = (index[:, None] * index[None, :] % NR) * (2.0 * math.pi / NR)
    return np.stack([np.cos(angle), -np.sin(angle)]).astype(np.float32)


def ring_send(x, axis, step):
    return lax.ppermute(x, axis, [(k, (k + step) % RING) for k in range(RING)])


def steering_rows(angle_ref, weights):
    factor = float(PSUB) ** -0.5
    rows = lax.broadcasted_iota(jnp.int32, (128, 256), 0)
    cols = lax.broadcasted_iota(jnp.int32, (128, 256), 1)
    spread = jnp.where(cols // 2 == rows, 1.0, 0.0).astype(BF)
    angle = angle_ref[...]
    cosine = (jnp.cos(angle) * factor).astype(BF)
    sine = (jnp.sin(angle) * factor).astype(BF)
    cosine = jnp.dot(cosine, spread, preferred_element_type=F4)
    sine = jnp.dot(sine, spread, preferred_element_type=F4)
    even = cols % 2 == 0
    weights[0] = jnp.where(even, cosine, -sine)
    weights[1] = jnp.where(even, sine, cosine)


def beam_matrix(weights, owners, z_first):
    y = lax.axis_index("y_hi") * 2 + lax.axis_index("y_lo")
    z = lax.axis_index("z")
    picked = []
    for first, second in owners:
        y_step, z_step = (second, first) if z_first else (first, second)
        y_of, z_of = lax.rem(y + y_step, RING), lax.rem(z + z_step, RING)
        block = lax.div(y_of, 2) * 8 + z_of * 2 + lax.rem(y_of, 2)
        start = pl.multiple_of(block * NB0, NB0)
        picked.append(weights[0, pl.ds(start, NB0), :])
        picked.append(weights[1, pl.ds(start, NB0), :])
    return jnp.concatenate(picked, 0).astype(BF)


def opening_kernel(angle_ref, raw_ref, *refs):
    outs, (weights, landed, angle_landed, sems) = refs[:4], refs[4:]
    angle_read = pltpu.make_async_copy(angle_ref, angle_landed, sems.at[READS])
    angle_read.start()

    def read(k):
        cols = pl.ds(k * READ, READ)
        return pltpu.make_async_copy(raw_ref.at[:, :, cols], landed.at[k], sems.at[k])

    for k in range(READS):
        read(k).start()
    angle_read.wait()
    steering_rows(angle_landed, weights)
    for k in range(READS):
        half = k // (READS // 2)
        matrix = beam_matrix(weights, SENT, half == 0)
        read(k).wait()
        base = k * READ - half * HALF
        for part in range(READ // STEP):
            raw = landed[k, :, :, part * STEP : (part + 1) * STEP].reshape(256, STEP)
            total = jnp.dot(matrix, raw, preferred_element_type=F4).astype(BF)
            cols = slice(base + part * STEP, base + (part + 1) * STEP)
            outs[2 * half][:, cols] = total[:64]
            outs[2 * half + 1][:, cols] = total[64:]


def opening_sums(angles, raw):
    vmem = pl.BlockSpec(memory_space=pltpu.VMEM)
    outs = [jax.ShapeDtypeStruct((n, HALF), BF) for n in SENT_ROWS * 2]
    outs += [jax.ShapeDtypeStruct((2, 128, 256), F4)]
    results = pl.pallas_call(
        opening_kernel,
        in_specs=[pl.BlockSpec(memory_space=pltpu.HBM)] * 2,
        out_specs=[vmem] * 5,
        out_shape=outs,
        scratch_shapes=[
            pltpu.VMEM((READS, 128, 2, READ), BF),
            pltpu.VMEM((128, 128), F4),
            pltpu.SemaphoreType.DMA((READS + 1,)),
        ],
        compiler_params=params(20),
        name="opening_sums",
    )(*(pltpu.with_memory_space_constraint(a, pltpu.HBM) for a in (angles, raw)))
    return results[:2], results[2:4], results[4]


def later_kernel(weights, raw_ref, *outs):
    steps = pl.num_programs(0) // 2
    for half in range(2):

        @pl.when(pl.program_id(0) // steps == half)
        def _():
            matrix = beam_matrix(weights, KEPT, half == 0)
            raw = raw_ref[...].reshape(256, READ)
            total = jnp.dot(matrix, raw, preferred_element_type=F4).astype(BF)
            step = lax.rem(pl.program_id(0), steps)
            cols = pl.ds(pl.multiple_of(step * READ, READ), READ)
            start = 0
            for out in outs[3 * half : 3 * half + 3]:
                size = out.shape[0]
                out[:, cols] = total[start : start + size]
                start += size


def later_sums(weights, raw):
    vmem = pl.BlockSpec(memory_space=pltpu.VMEM)
    outs = [jax.ShapeDtypeStruct((n, HALF), BF) for n in KEPT_ROWS * 2]
    kept = pl.pallas_call(
        later_kernel,
        grid=(READS,),
        in_specs=[vmem, pl.BlockSpec((128, 2, READ), lambda i: (0, 0, i))],
        out_specs=[vmem] * 6,
        out_shape=outs,
        compiler_params=params(20),
        name="later_sums",
    )(weights, pltpu.with_memory_space_constraint(raw, pltpu.HBM))
    return kept[:3], kept[3:]


def relay(q, received):
    rows = q.shape[0]
    return (q.astype(F4) + received[:rows].astype(F4)).astype(BF)


def middle_kernel(own, p1, m1, p2, m2, plus, minus, q1, q3, keep):
    tile = 512

    def step(k, carry):
        cols = pl.ds(pl.multiple_of(k * tile, tile), tile)
        low = own[:32, cols].astype(F4) + m1[32:, cols].astype(F4) + p2[:, cols].astype(F4)
        high = own[32:, cols].astype(F4) + p1[32:, cols].astype(F4) + m2[:, cols].astype(F4)
        keep[:, cols] = low[:16]
        q1[:, cols] = low[16:24].astype(BF)
        plus[:, cols] = jnp.concatenate([high[:8], low[24:]], 0).astype(BF)
        minus[:, cols] = jnp.concatenate([high[8:16], high[16:24]], 0).astype(BF)
        q3[:, cols] = high[24:].astype(BF)
        return carry

    lax.fori_loop(0, HALF // tile, step, 0)


def middle_sums(own, p1, m1, p2, m2):
    outs = ((16, BF), (16, BF), (8, BF), (8, BF), (16, F4))
    vmem = pl.BlockSpec(memory_space=pltpu.VMEM)
    return pl.pallas_call(
        middle_kernel,
        in_specs=[vmem] * 5,
        out_specs=[vmem] * 5,
        out_shape=[jax.ShapeDtypeStruct((n, HALF), d) for n, d in outs],
        compiler_params=params(4),
        name="middle_sums",
    )(own, p1, m1, p2, m2)


def compress_kernel(*refs):
    ins, (form_ref, turn_ref, filter_ref, out, lines, bins) = refs[:10], refs[10:]
    for half in range(2):
        keep, p3, m3, p4, m4 = ins[5 * half : 5 * half + 5]
        sums = (
            keep[:8] + m3[...].astype(F4)[8:] + p4[...].astype(F4),
            keep[8:] + p3[...].astype(F4)[8:] + m4[...].astype(F4),
        )
        for part in range(2):
            for k in range(64):
                row = (half * 64 + k) * 8
                lines[part, row : row + 8, :] = sums[part][:, k * 128 : (k + 1) * 128]
    form = form_ref[...]
    cos_part, sin_part = turn_ref[0], turn_ref[1]
    scale = NR ** (-0.5)
    real_filter, imag_filter = filter_ref[0] * scale, filter_ref[1] * scale
    for beam in range(NB0):
        picked = pl.ds(beam, 128, stride=8)
        data = jnp.concatenate([lines[0, picked, :], lines[1, picked, :]], 0)
        upper = data.astype(BF)
        lower = (data - upper.astype(F4)).astype(BF)
        one = jnp.dot(form, jnp.concatenate([upper, lower], 1), preferred_element_type=F4)
        one = one[:, :128] + one[:, 128:]
        real_in, imag_in = one[:128], one[128:]
        turned = jnp.concatenate(
            [real_in * cos_part - imag_in * sin_part, real_in * sin_part + imag_in * cos_part], 1
        )
        upper = turned.astype(BF)
        lower = (turned - upper.astype(F4)).astype(BF)
        two = lax.dot_general(
            form,
            jnp.concatenate([upper, lower], 0),
            (((1,), (1,)), ((), ())),
            preferred_element_type=F4,
        )
        two = two[:, :128] + two[:, 128:]
        real_in, imag_in = two[:128], two[128:]
        bins[0, picked, :] = real_in * real_filter - imag_in * imag_filter
        bins[1, picked, :] = real_in * imag_filter + imag_in * real_filter
    for slab in range(8):
        for k in range(16):
            row = (slab * 16 + k) * 8
            both = jnp.concatenate([bins[0, row : row + 8, :], bins[1, row : row + 8, :]], 0)
            out[slab, :, k * 128 : (k + 1) * 128] = both.astype(BF)


def compressed_beams(pieces, range_filter):
    return pl.pallas_call(
        compress_kernel,
        out_shape=jax.ShapeDtypeStruct((8, 16, SLAB), BF),
        scratch_shapes=[pltpu.VMEM((2, 1024, 128), F4), pltpu.VMEM((2, 1024, 128), F4)],
        compiler_params=params(12),
        name="compressed_beams",
    )(
        *pieces,
        jnp.asarray(real_form_transposed()),
        jnp.asarray(twiddle()),
        range_filter.reshape(2, 128, 128),
    )


def sided(near, far, direct):
    if direct:
        return near, far
    even = lax.axis_index("y_lo") == 0
    return jnp.where(even, far, near), jnp.where(even, near, far)


def table_kernel(direct, start_ref, own_ref, near_ref, far_ref, *refs):
    matrix, near_a, near_b, far_cos, far_sin, lines = refs

    def columns(fields):
        padded = jnp.concatenate([fields, jnp.zeros((112, 256), F4)], 0)
        return jnp.concatenate([padded[:, :128].T, padded[:, 128:].T], 0)

    def joined(ref):
        parts = ref[0].astype(F4)
        return parts[:, :256] + parts[:, 256:512] + parts[:, 512:768]

    left, right = sided(joined(near_ref), joined(far_ref), direct)
    own, left, right = columns(own_ref[...]), columns(left), columns(right)

    def piece(source, side, first, count, shift):
        rows = source[side * 128 + first : side * 128 + first + count]
        field = lax.broadcasted_iota(jnp.int32, rows.shape, 1)
        return rows + jnp.where(field == 0, float(shift), 0.0)

    for side in range(2):
        row = side * SIDE
        for source, first, count, shift in (
            (left, 8, 8, 0),
            (own, 0, 16, 8),
            (right, 0, 8, 16),
            (left, 40, 8, -8),
            (own, 16, 32, 8),
            (right, 16, 8, 24),
        ):
            lines[row : row + count, :] = piece(source, side, first, count, shift)
            row += count
        for twin in range(2):
            lines[pl.ds(row + twin, 64, stride=2), :] = piece(own, side, 48, 64, 8)
    rows = 2 * SIDE
    lane = lax.broadcasted_iota(jnp.int32, (rows, 128), 1)
    row = lax.broadcasted_iota(jnp.int32, (rows, 128), 0) % SIDE
    lane_f = lane.astype(F4)
    table = lines[...]
    offset = table[:, 0:1]
    total = jnp.zeros((rows, 128), F4)
    for tap in range(BAND):
        total = total + jnp.where(lane_f == offset + float(tap), table[:, tap + 1 : tap + 2], 0.0)
    matrix[...] = total
    delay = table[:, 9:10]
    step = delay * (lane_f * (1.0 / NR))
    far_cos[...] = jnp.cos(step)
    far_sin[...] = jnp.sin(step)
    first = start_ref[0].astype(F4)
    base = delay * (1.0 + (first + lane_f * 128.0) * (1.0 / NR))
    cosine, sine = jnp.cos(base), jnp.sin(base)
    odd = (row >= 80) & (row % 2 == 1)
    value_a = jnp.where(odd, sine, cosine)
    value_b = jnp.where(odd, cosine, -sine)
    for tile in range(SLAB // COLS):
        lanes = slice(tile * 4, tile * 4 + 4)
        near_a[tile, :, 0:4] = value_a[:, lanes]
        near_b[tile, :, 0:4] = value_b[:, lanes]


def merge_tables(start, own, near, far, direct):
    rows = 2 * SIDE
    tiles = SLAB // COLS
    one = jax.ShapeDtypeStruct((rows, 128), F4)
    many = jax.ShapeDtypeStruct((tiles, rows, 128), F4)
    vmem = pl.BlockSpec(memory_space=pltpu.VMEM)
    packed = pl.BlockSpec((1, 16, PIECE), lambda i: (8, 0, 0))
    return pl.pallas_call(
        functools.partial(table_kernel, direct),
        grid=(1,),
        in_specs=[pl.BlockSpec(memory_space=pltpu.SMEM), vmem, packed, packed],
        out_specs=[vmem] * 5,
        out_shape=[one, many, many, one, one],
        scratch_shapes=[pltpu.VMEM((rows, 128), F4)],
        compiler_params=params(12),
        name="merge_tables",
    )(start, own, near, far)


def split_rows(matrix):
    upper = matrix.astype(BF)
    return upper, (matrix - upper.astype(F4)).astype(BF)


def merge_kernel(direct, near, own, far, matrix, near_a, near_b, far_cos, far_sin, *refs):
    out = refs[-1]
    dot = functools.partial(jnp.dot, preferred_element_type=F4)

    def phases(first, count):
        rows = slice(first, first + count)
        cosine, sine = far_cos[rows, :], far_sin[rows, :]
        real_parts, imag_parts = [], []
        for k in range(COLS // 128):
            a, b = near_a[0, rows, k : k + 1], near_b[0, rows, k : k + 1]
            real_parts.append(a * cosine + b * sine)
            imag_parts.append(b * cosine - a * sine)
        return jnp.concatenate(real_parts, 1), jnp.concatenate(imag_parts, 1)

    def blend(matrices, image, exact):
        upper, lower = matrices
        rows = upper.shape[0]
        if exact:
            both = dot(jnp.concatenate([upper, lower], 0), image.astype(BF))
            return both[:rows] + both[rows:]
        high = image.astype(BF)
        low = (image - high.astype(F4)).astype(BF)
        both = dot(jnp.concatenate([upper, lower], 0), high)
        return both[:rows] + both[rows:] + dot(upper, low)

    zeros = jnp.zeros((8, COLS), F4)
    images = []
    for side in range(8):
        left, right = sided(near[side].astype(F4), far[side].astype(F4), direct)
        parts = (left, own[side].astype(F4), right)
        images.append(
            tuple(jnp.concatenate([p[8 * q : 8 * q + 8] for p in parts] + [zeros], 0) for q in (0, 1))
        )
    for first, count, depth in ((0, 32, 32), (32, 48, 32)):
        sides = [
            (
                split_rows(matrix[c * SIDE + first : c * SIDE + first + count, :depth]),
                phases(c * SIDE + first, count),
            )
            for c in range(2)
        ]
        merged = []
        for group in range(len(images) // 2):
            real_sum, imag_sum = None, None
            for c, (matrices, (a, b)) in enumerate(sides):
                real_in, imag_in = (
                    blend(matrices, images[2 * group + c][q], first == 0) for q in (0, 1)
                )
                real_out = a * real_in + b * imag_in
                imag_out = a * imag_in - b * real_in
                real_sum = real_out if c == 0 else real_sum + real_out
                imag_sum = imag_out if c == 0 else imag_sum + imag_out
            merged.append((real_sum, imag_sum))
        images = merged
    total = None
    for c in range(2):
        rows = slice(c * SIDE + 80, c * SIDE + SIDE)
        matrices = split_rows(matrix[rows, :48])
        a, b = phases(c * SIDE + 80, 128)
        value = a * blend(matrices, images[c][0], False) + b * blend(matrices, images[c][1], False)
        total = value if c == 0 else total + value
    out[...] = total.reshape(64, 2, COLS)


def merge(near, own, far, tables, piece, direct, so_far):
    matrix, near_a, near_b, far_cos, far_sin = tables
    rows = matrix.shape[0]
    steps = PIECE // COLS
    first = piece * steps
    image = pl.BlockSpec((8, 16, COLS), lambda i: (0, 0, i))
    whole = pl.BlockSpec((rows, 128), lambda i: (0, 0))
    tiled = pl.BlockSpec((1, rows, 128), lambda i: (first + i, 0, 0))
    return pl.pallas_call(
        functools.partial(merge_kernel, direct),
        grid=(steps,),
        in_specs=[image, pl.BlockSpec((8, 16, COLS), lambda i: (0, 0, first + i)), image]
        + [whole, tiled, tiled, whole, whole]
        + [pl.BlockSpec(memory_space=pl.ANY)] * len(so_far),
        out_specs=pl.BlockSpec((64, 2, COLS), lambda i: (0, 0, first + i)),
        out_shape=jax.ShapeDtypeStruct((64, 2, SLAB), F4),
        input_output_aliases={8: 0} if so_far else {},
        compiler_params=params(24),
        name="merge",
    )(near, own, far, matrix, near_a, near_b, far_cos, far_sin, *so_far)


def from_neighbours(array, direct):
    blocks = lax.axis_size(BEAM_COMP)
    if direct:
        steps = [(k, k + 1) for k in range(blocks - 1)]
        left = lax.ppermute(array, BEAM_COMP, steps)
        right = lax.ppermute(array, BEAM_COMP, [(b, a) for a, b in steps])
        return left, right
    near = lax.ppermute(array, BEAM_COMP, [(k, k ^ 1) for k in range(blocks)])
    steps = [(k, k + 2 - 4 * (k % 2)) for k in range(blocks)]
    far = lax.ppermute(near, BEAM_COMP, [(a, b) for a, b in steps if 0 <= b < blocks])
    return near, far


def own_table(band_offsets, band_weights, beam_delay):
    fields = jnp.concatenate(
        [
            band_offsets.astype(F4)[None],
            jnp.moveaxis(band_weights, 2, 0),
            beam_delay[None],
        ],
        0,
    )
    return jnp.pad(fields, ((0, 6), (0, 0), (0, 16))).reshape(16, 256)


def packed_table(table):
    parts = []
    for _ in range(3):
        part = lax.reduce_precision(table, 8, 7)
        parts.append(part.astype(BF))
        table = table - part
    return jnp.pad(jnp.concatenate(parts, 1), ((0, 0), (0, PIECE - 768)))[None]


def ring_start(parts, first):
    return ring_send(parts[0], first, 1), ring_send(parts[1], first, -1)


def ring_rest(kept, received, first, second):
    q1, q3, own = kept
    p1, m1 = received
    p2 = ring_send(relay(q1, p1), first, 1)
    m2 = ring_send(relay(q3, m1), first, -1)
    plus, minus, q1, q3, keep = middle_sums(own, p1, m1, p2, m2)
    p3 = ring_send(plus, second, 1)
    m3 = ring_send(minus, second, -1)
    p4 = ring_send(relay(q1, p3), second, 1)
    m4 = ring_send(relay(q3, m3), second, -1)
    return keep, p3, m3, p4, m4


def body(raw_pulses, range_filter, steer_angle, band_offsets, band_weights, beam_delay):
    sent_z, sent_y, weights = opening_sums(steer_angle, raw_pulses)
    received_z = ring_start(sent_z, Z)
    received_y = ring_start(sent_y, Y)
    table = own_table(band_offsets, band_weights, beam_delay)
    packed = packed_table(table)
    kept_z, kept_y = later_sums(weights, raw_pulses)
    start = (lax.axis_index("sub") * SLAB).astype(jnp.int32).reshape(1)
    pieces = ring_rest(kept_z, received_z, Z, Y)
    pieces += ring_rest(kept_y, received_y, Y, Z)
    beams = compressed_beams(pieces, range_filter)
    image = lax.all_to_all(beams, "sub", 0, 0, tiled=True)
    scene = ()
    for piece in range(PIECES):
        direct = DIRECT[piece]
        message = image[:, :, piece * PIECE : (piece + 1) * PIECE]
        if piece == 0:
            message = jnp.concatenate([message, packed], 0)
        near, far = from_neighbours(message, direct)
        if piece == 0:
            tables = merge_tables(start, table, near, far, direct)
        scene = (merge(near, image, far, tables, piece, direct, scene),)
    return scene[0]


def solution(mesh):
    split = Mesh(
        mesh.devices.reshape(mesh.shape["sub"], 2, RING, mesh.shape["comp"]), SUB_BEAM_COMP
    )
    return jax.shard_map(
        body,
        mesh=split,
        in_specs=(
            P(SUB_BEAM_COMP, None, None),
            P(),
            P(None, SUB_BEAM_COMP),
            P(None, BEAM_COMP),
            P(None, BEAM_COMP, None),
            P(None, BEAM_COMP),
        ),
        out_specs=P(BEAM_COMP, None, "sub"),
        check_vma=False,
    )
```

```python
import functools
import math

import jax
import jax.numpy as jnp
import ml_dtypes
import numpy as np
from jax import lax
from jax.experimental import pallas as pl
from jax.experimental.pallas import tpu as pltpu
from jax.sharding import Mesh
from jax.sharding import PartitionSpec as P

NR = 16384
RADIX = 128
NB0 = 8
BAND = 8
PSUB = 2048
RING = 4
HALF = NR // 2
READS = 4
READ = NR // READS
STEP = 2048
SLAB = NR // 8
COLS = 512
FIELDS = 256
SIDE = 144
BEAM_COMP = ("y_hi", "z", "y_lo")
SUB_BEAM_COMP = ("sub", "y_hi", "z", "y_lo")
Y = ("y_hi", "y_lo")
Z = "z"
BF = jnp.bfloat16
F4 = jnp.float32
SENT = ((2, 0), (2, 1), (1, 2), (1, 3), (2, 2), (2, 3), (3, 0), (3, 1))
KEPT = ((1, 0), (1, 1), (3, 2), (3, 3), (0, 0), (0, 1), (0, 2), (0, 3))
KEPT_ROWS = (32, 32, 64)


def params(mebibytes):
    return pltpu.CompilerParams(vmem_limit_bytes=mebibytes << 20)


def real_form_transposed():
    index = np.arange(RADIX)
    angle = (index[:, None] * index[None, :] % RADIX) * (2.0 * math.pi / RADIX)
    cos_part, sin_part = np.cos(angle), -np.sin(angle)
    upper = np.concatenate([cos_part, sin_part], 1)
    lower = np.concatenate([-sin_part, cos_part], 1)
    return np.concatenate([upper, lower], 0).T.astype(ml_dtypes.bfloat16)


def twiddle():
    index = np.arange(RADIX)
    angle = (index[:, None] * index[None, :] % NR) * (2.0 * math.pi / NR)
    return np.stack([np.cos(angle), -np.sin(angle)]).astype(np.float32)


def ring_send(x, axis, step):
    return lax.ppermute(x, axis, [(k, (k + step) % RING) for k in range(RING)])


def steering_rows(angle_ref, weights):
    factor = float(PSUB) ** -0.5
    rows = lax.broadcasted_iota(jnp.int32, (128, 256), 0)
    cols = lax.broadcasted_iota(jnp.int32, (128, 256), 1)
    spread = jnp.where(cols // 2 == rows, 1.0, 0.0).astype(BF)
    angle = angle_ref[...]
    cosine = (jnp.cos(angle) * factor).astype(BF)
    sine = (jnp.sin(angle) * factor).astype(BF)
    cosine = jnp.dot(cosine, spread, preferred_element_type=F4)
    sine = jnp.dot(sine, spread, preferred_element_type=F4)
    even = cols % 2 == 0
    weights[0] = jnp.where(even, cosine, -sine)
    weights[1] = jnp.where(even, sine, cosine)


def beam_matrix(weights, owners, z_first):
    y = lax.axis_index("y_hi") * 2 + lax.axis_index("y_lo")
    z = lax.axis_index("z")
    picked = []
    for first, second in owners:
        y_step, z_step = (second, first) if z_first else (first, second)
        y_of, z_of = lax.rem(y + y_step, RING), lax.rem(z + z_step, RING)
        block = lax.div(y_of, 2) * 8 + z_of * 2 + lax.rem(y_of, 2)
        start = pl.multiple_of(block * NB0, NB0)
        picked.append(weights[0, pl.ds(start, NB0), :])
        picked.append(weights[1, pl.ds(start, NB0), :])
    return jnp.concatenate(picked, 0).astype(BF)


def split_three(table):
    parts = []
    for _ in range(3):
        part = table.astype(BF)
        parts.append(part)
        table = table - part.astype(F4)
    return parts


def opening_kernel(angle_ref, offset_ref, band_ref, delay_ref, raw_ref, *refs):
    outs, (weights, table) = refs[:4], refs[4:6]
    landed, angle_landed, offset_landed, band_landed, delay_landed, sems = refs[6:]
    small = (
        (angle_ref, angle_landed),
        (offset_ref, offset_landed),
        (band_ref, band_landed),
        (delay_ref, delay_landed),
    )
    small_reads = [
        pltpu.make_async_copy(source, target, sems.at[READS + k])
        for k, (source, target) in enumerate(small)
    ]
    for copy in small_reads:
        copy.start()

    def read(k):
        cols = pl.ds(k * READ, READ)
        return pltpu.make_async_copy(raw_ref.at[:, :, cols], landed.at[k], sems.at[k])

    for k in range(READS):
        read(k).start()
    for copy in small_reads:
        copy.wait()
    steering_rows(angle_landed, weights)
    width = offset_landed.shape[1]
    table[...] = jnp.zeros_like(table)
    for side in range(2):
        cols = slice(side * 128, side * 128 + width)
        table[0:1, cols] = offset_landed[side : side + 1, :].astype(F4)
        table[1:9, cols] = band_landed[side]
        table[9:10, cols] = delay_landed[side : side + 1, :]
    parts = split_three(table[...])
    packed = jnp.concatenate([*parts, jnp.zeros_like(parts[0])], 0)
    for out in outs[2:]:
        out[:, HALF:] = packed
    for k in range(READS):
        half = k // (READS // 2)
        matrix = beam_matrix(weights, SENT, half == 0)
        read(k).wait()
        base = k * READ - half * HALF
        for part in range(READ // STEP):
            raw = landed[k, :, :, part * STEP : (part + 1) * STEP].reshape(256, STEP)
            total = jnp.dot(matrix, raw, preferred_element_type=F4).astype(BF)
            cols = slice(base + part * STEP, base + (part + 1) * STEP)
            outs[2 * half][:, cols] = total[:64]
            outs[2 * half + 1][:, cols] = total[64:]


def opening_sums(raw, *small):
    vmem = pl.BlockSpec(memory_space=pltpu.VMEM)
    outs = [jax.ShapeDtypeStruct((64, c), BF) for c in (HALF, HALF, HALF + FIELDS, HALF + FIELDS)]
    outs += [jax.ShapeDtypeStruct((2, 128, 256), F4), jax.ShapeDtypeStruct((16, FIELDS), F4)]
    results = pl.pallas_call(
        opening_kernel,
        in_specs=[pl.BlockSpec(memory_space=pltpu.HBM)] * 5,
        out_specs=[vmem] * 6,
        out_shape=outs,
        scratch_shapes=[pltpu.VMEM((READS, 128, 2, READ), BF)]
        + [pltpu.VMEM(array.shape, array.dtype) for array in small]
        + [pltpu.SemaphoreType.DMA((READS + 4,))],
        compiler_params=params(20),
        name="opening_sums",
    )(*(pltpu.with_memory_space_constraint(a, pltpu.HBM) for a in (*small, raw)))
    return results[:2], results[2:4], *results[4:]


def later_kernel(weights, raw_ref, *outs):
    steps = pl.num_programs(0) // 2
    for half in range(2):

        @pl.when(pl.program_id(0) // steps == half)
        def _():
            matrix = beam_matrix(weights, KEPT, half == 0)
            raw = raw_ref[...].reshape(256, READ)
            total = jnp.dot(matrix, raw, preferred_element_type=F4).astype(BF)
            step = lax.rem(pl.program_id(0), steps)
            cols = pl.ds(pl.multiple_of(step * READ, READ), READ)
            start = 0
            for out in outs[3 * half : 3 * half + 3]:
                size = out.shape[0]
                out[:, cols] = total[start : start + size]
                start += size


def later_sums(weights, raw):
    vmem = pl.BlockSpec(memory_space=pltpu.VMEM)
    outs = [jax.ShapeDtypeStruct((n, HALF), BF) for n in KEPT_ROWS * 2]
    kept = pl.pallas_call(
        later_kernel,
        grid=(READS,),
        in_specs=[vmem, pl.BlockSpec((128, 2, READ), lambda i: (0, 0, i))],
        out_specs=[vmem] * 6,
        out_shape=outs,
        compiler_params=params(20),
        name="later_sums",
    )(weights, pltpu.with_memory_space_constraint(raw, pltpu.HBM))
    return kept[:3], kept[3:]


def relay(q, received):
    rows, cols = q.shape
    return (q.astype(F4) + received[:rows, :cols].astype(F4)).astype(BF)


def middle_kernel(own, p1, m1, p2, m2, plus, minus, q1, q3, keep):
    tile = 512

    def step(k, carry):
        cols = pl.ds(pl.multiple_of(k * tile, tile), tile)
        low = own[:32, cols].astype(F4) + m1[32:, cols].astype(F4) + p2[:, cols].astype(F4)
        high = own[32:, cols].astype(F4) + p1[32:, cols].astype(F4) + m2[:, cols].astype(F4)
        keep[:, cols] = low[:16]
        q1[:, cols] = low[16:24].astype(BF)
        plus[:, cols] = jnp.concatenate([high[:8], low[24:]], 0).astype(BF)
        minus[:, cols] = jnp.concatenate([high[8:16], high[16:24]], 0).astype(BF)
        q3[:, cols] = high[24:].astype(BF)
        return carry

    lax.fori_loop(0, HALF // tile, step, 0)
    if plus.shape[1] > HALF:
        for j, received in enumerate((p1, m1)):
            for k in range(3):
                first = HALF + (3 * j + k) * FIELDS
                part = received[16 * k : 16 * k + 16, HALF:]
                plus[:, first : first + FIELDS] = part
                minus[:, first : first + FIELDS] = part


def middle_sums(own, p1, m1, p2, m2):
    wide = HALF + 6 * (p1.shape[1] - HALF)
    outs = ((16, wide, BF), (16, wide, BF), (8, HALF, BF), (8, HALF, BF), (16, HALF, F4))
    vmem = pl.BlockSpec(memory_space=pltpu.VMEM)
    return pl.pallas_call(
        middle_kernel,
        in_specs=[vmem] * 5,
        out_specs=[vmem] * 5,
        out_shape=[jax.ShapeDtypeStruct((n, c), d) for n, c, d in outs],
        compiler_params=params(4),
        name="middle_sums",
    )(own, p1, m1, p2, m2)


def compress_kernel(*refs):
    ins, (form_ref, turn_ref, filter_ref, out, lines, bins) = refs[:10], refs[10:]
    for half in range(2):
        keep, p3, m3, p4, m4 = ins[5 * half : 5 * half + 5]
        sums = (
            keep[:8] + m3[:, :HALF].astype(F4)[8:] + p4[...].astype(F4),
            keep[8:] + p3[:, :HALF].astype(F4)[8:] + m4[...].astype(F4),
        )
        for part in range(2):
            for k in range(64):
                row = (half * 64 + k) * 8
                lines[part, row : row + 8, :] = sums[part][:, k * 128 : (k + 1) * 128]
    form = form_ref[...]
    cos_part, sin_part = turn_ref[0], turn_ref[1]
    scale = NR ** (-0.5)
    real_filter, imag_filter = filter_ref[0] * scale, filter_ref[1] * scale
    for beam in range(NB0):
        picked = pl.ds(beam, 128, stride=8)
        data = jnp.concatenate([lines[0, picked, :], lines[1, picked, :]], 0)
        upper = data.astype(BF)
        lower = (data - upper.astype(F4)).astype(BF)
        one = jnp.dot(form, jnp.concatenate([upper, lower], 1), preferred_element_type=F4)
        one = one[:, :128] + one[:, 128:]
        real_in, imag_in = one[:128], one[128:]
        turned = jnp.concatenate(
            [real_in * cos_part - imag_in * sin_part, real_in * sin_part + imag_in * cos_part], 1
        )
        upper = turned.astype(BF)
        lower = (turned - upper.astype(F4)).astype(BF)
        two = lax.dot_general(
            form,
            jnp.concatenate([upper, lower], 0),
            (((1,), (1,)), ((), ())),
            preferred_element_type=F4,
        )
        two = two[:, :128] + two[:, 128:]
        real_in, imag_in = two[:128], two[128:]
        bins[0, picked, :] = real_in * real_filter - imag_in * imag_filter
        bins[1, picked, :] = real_in * imag_filter + imag_in * real_filter
    for slab in range(8):
        for k in range(16):
            row = (slab * 16 + k) * 8
            both = jnp.concatenate([bins[0, row : row + 8, :], bins[1, row : row + 8, :]], 0)
            out[slab, :, k * 128 : (k + 1) * 128] = both.astype(BF)


def compressed_beams(pieces, range_filter):
    return pl.pallas_call(
        compress_kernel,
        out_shape=jax.ShapeDtypeStruct((8, 16, SLAB), BF),
        scratch_shapes=[pltpu.VMEM((2, 1024, 128), F4), pltpu.VMEM((2, 1024, 128), F4)],
        compiler_params=params(12),
        name="compressed_beams",
    )(
        *pieces,
        jnp.asarray(real_form_transposed()),
        jnp.asarray(twiddle()),
        range_filter.reshape(2, 128, 128),
    )


def sided(near, far):
    even = lax.axis_index("y_lo") == 0
    return jnp.where(even, far, near), jnp.where(even, near, far)


def table_kernel(start_ref, own_ref, y_below, y_above, z_below, z_above, *refs):
    matrix, near_cos, near_sin, far_cos, far_sin, lines = refs
    y_hi, z = lax.axis_index("y_hi"), lax.axis_index("z")
    even = lax.axis_index("y_lo") == 0

    def columns(fields):
        padded = jnp.concatenate([fields, jnp.zeros((112, 256), F4)], 0)
        return jnp.concatenate([padded[:, :128].T, padded[:, 128:].T], 0)

    def from_rows(ref):
        parts = ref[:48, HALF:].astype(F4)
        return parts[:16] + parts[16:32] + parts[32:]

    def from_cols(ref, j):
        first = HALF + 3 * j * FIELDS
        parts = ref[:, first : first + 3 * FIELDS].astype(F4)
        return parts[:, :256] + parts[:, 256:512] + parts[:, 512:]

    near = jnp.where(even, from_rows(y_above), from_rows(y_below))
    left = jnp.where(z > 0, from_cols(z_below, 1), from_cols(z_below, 0))
    right = jnp.where(z < RING - 1, from_cols(z_above, 0), from_cols(z_above, 1))
    left = jnp.where((z > 0) | (y_hi > 0), left, 0.0)
    right = jnp.where((z < RING - 1) | (y_hi == 0), right, 0.0)
    left, right = sided(near, jnp.where(even, left, right))
    own, left, right = columns(own_ref[...]), columns(left), columns(right)

    def piece(source, side, first, count, shift):
        rows = source[side * 128 + first : side * 128 + first + count]
        field = lax.broadcasted_iota(jnp.int32, rows.shape, 1)
        return rows + jnp.where(field == 0, float(shift), 0.0)

    for side in range(2):
        row = side * SIDE
        for source, first, count, shift in (
            (left, 8, 8, 0),
            (own, 0, 16, 8),
            (right, 0, 8, 16),
            (left, 40, 8, -8),
            (own, 16, 32, 8),
            (right, 16, 8, 24),
            (own, 48, 64, 8),
        ):
            lines[row : row + count, :] = piece(source, side, first, count, shift)
            row += count
    rows = 2 * SIDE
    table = lines[...]
    lane = lax.broadcasted_iota(jnp.int32, (rows, 256), 1)
    row = lax.broadcasted_iota(jnp.int32, (rows, 256), 0) % SIDE
    depth = jnp.where(row < 80, 32, 48)
    term = lane // depth
    place = (lane - term * depth).astype(F4) - table[:, 0:1]
    band = jnp.zeros((rows, 256), F4)
    for tap in range(BAND):
        band = band + jnp.where(place == float(tap), table[:, tap + 1 : tap + 2], 0.0)
    upper = band.astype(BF).astype(F4)
    matrix[...] = jnp.where(term == 1, band - upper, upper).astype(BF)
    delay = table[:, 9:10]
    lane = lax.broadcasted_iota(jnp.int32, (rows, 128), 1).astype(F4)
    step = delay * (lane * (1.0 / NR))
    far_cos[...] = jnp.cos(step)
    far_sin[...] = jnp.sin(step)
    first = start_ref[0].astype(F4)
    base = delay * (1.0 + (first + lane * 128.0) * (1.0 / NR))
    near_cos[...] = jnp.cos(base)
    near_sin[...] = jnp.sin(base)


def merge_tables(start, own, *received):
    rows = 2 * SIDE
    vmem = pl.BlockSpec(memory_space=pltpu.VMEM)
    return pl.pallas_call(
        table_kernel,
        grid=(1,),
        in_specs=[pl.BlockSpec(memory_space=pltpu.SMEM)] + [vmem] * 5,
        out_specs=[pl.BlockSpec((rows, 256), lambda i: (0, 0))]
        + [pl.BlockSpec((rows, 128), lambda i: (0, 0))] * 4,
        out_shape=[pltpu.HBM((rows, 256), BF)] + [pltpu.HBM((rows, 128), F4)] * 4,
        scratch_shapes=[pltpu.VMEM((rows, 128), F4)],
        compiler_params=params(12),
        name="merge_tables",
    )(start, own, *received)


def merge_kernel(near, own, far, matrix, near_cos, near_sin, far_cos, far_sin, out, lines):
    groups = COLS // 128
    shift = lax.rem(128 - groups * pl.program_id(0), 128)
    cosines = pltpu.roll(near_cos[...], shift, 1)
    sines = pltpu.roll(near_sin[...], shift, 1)

    def phases(first, count):
        rows = slice(first, first + count)
        cosine, sine = far_cos[rows, :], far_sin[rows, :]
        real_parts, imag_parts = [], []
        for k in range(groups):
            a, b = cosines[rows, k : k + 1], sines[rows, k : k + 1]
            real_parts.append(a * cosine - b * sine)
            imag_parts.append(b * cosine + a * sine)
        return jnp.concatenate(real_parts, 1), jnp.concatenate(imag_parts, 1)

    def stacked(image, exact):
        upper = image.astype(BF)
        if exact:
            return jnp.concatenate([upper, upper], 0)
        lower = (image - upper.astype(F4)).astype(BF)
        return jnp.concatenate([upper, upper, lower], 0)

    zeros = jnp.zeros((8, COLS), F4)
    images = []
    for sub in range(8):
        left, right = sided(near[sub].astype(F4), far[sub].astype(F4))
        parts = (left, own[sub].astype(F4), right)
        images.append(
            tuple(jnp.concatenate([p[8 * q : 8 * q + 8] for p in parts] + [zeros], 0) for q in (0, 1))
        )
    for first, count, terms in ((0, 32, 64), (32, 48, 96), (80, 64, 144)):
        merged = [None] * (len(images) // 2)
        for side in range(2):
            start = side * SIDE + first
            band = matrix[start : start + count, :terms]
            cosine, sine = phases(start, count)
            for group in range(len(merged)):
                real_in, imag_in = (
                    jnp.dot(band, stacked(part, first == 0), preferred_element_type=F4)
                    for part in images[2 * group + side]
                )
                real_out = cosine * real_in - sine * imag_in
                imag_out = sine * real_in + cosine * imag_in
                if side:
                    real_out, imag_out = merged[group][0] + real_out, merged[group][1] + imag_out
                merged[group] = (real_out, imag_out)
        images = merged
    for k in range(groups):
        cols = slice(k * 128, (k + 1) * 128)
        for part in range(2):
            lines[k, pl.ds(part, 64, stride=2), :] = images[0][part][:, cols]
        out[:, :, cols] = lines[k].reshape(64, 2, 128)


def merge(near, own, far, tables):
    rows = 2 * SIDE
    image = pl.BlockSpec((8, 16, COLS), lambda i: (0, 0, i))
    whole = pl.BlockSpec((rows, 128), lambda i: (0, 0))
    return pl.pallas_call(
        merge_kernel,
        grid=(SLAB // COLS,),
        in_specs=[image] * 3 + [pl.BlockSpec((rows, 256), lambda i: (0, 0))] + [whole] * 4,
        out_specs=pl.BlockSpec((64, 2, COLS), lambda i: (0, 0, i)),
        out_shape=jax.ShapeDtypeStruct((64, 2, SLAB), F4),
        scratch_shapes=[pltpu.VMEM((COLS // 128, 128, 128), F4)],
        compiler_params=params(16),
        name="merge",
    )(near, own, far, *(pltpu.with_memory_space_constraint(t, pltpu.HBM) for t in tables))


def from_near(array):
    blocks = lax.axis_size(BEAM_COMP)
    return lax.ppermute(array, BEAM_COMP, [(k, k ^ 1) for k in range(blocks)])


def from_far(array):
    blocks = lax.axis_size(BEAM_COMP)
    steps = [(k, k - 1 + 2 * (k % 2)) for k in range(1, blocks - 1)]
    return lax.ppermute(array, BEAM_COMP, steps)


def ring_start(parts, first):
    return ring_send(parts[0], first, 1), ring_send(parts[1], first, -1)


def ring_rest(kept, received, first, second):
    q1, q3, own = kept
    p1, m1 = received
    p2 = ring_send(relay(q1, p1), first, 1)
    m2 = ring_send(relay(q3, m1), first, -1)
    plus, minus, q1, q3, keep = middle_sums(own, p1, m1, p2, m2)
    p3 = ring_send(plus, second, 1)
    m3 = ring_send(minus, second, -1)
    p4 = ring_send(relay(q1, p3), second, 1)
    m4 = ring_send(relay(q3, m3), second, -1)
    return keep, p3, m3, p4, m4


def body(raw_pulses, range_filter, steer_angle, band_offsets, band_weights, beam_delay):
    sent_z, sent_y, weights, table = opening_sums(
        raw_pulses, steer_angle, band_offsets, jnp.moveaxis(band_weights, 2, 1), beam_delay
    )
    received_z = ring_start(sent_z, Z)
    received_y = ring_start(sent_y, Y)
    kept_z, kept_y = later_sums(weights, raw_pulses)
    start = (lax.axis_index("sub") * SLAB).astype(jnp.int32).reshape(1)
    pieces_z = ring_rest(kept_z, received_z, Z, Y)
    pieces_y = ring_rest(kept_y, received_y, Y, Z)
    tables = merge_tables(start, table, *received_y, *pieces_y[1:3])
    beams = compressed_beams(pieces_z + pieces_y, range_filter)
    near_beams = from_near(beams)
    image = lax.all_to_all(beams, "sub", 0, 0, tiled=True)
    near = lax.all_to_all(near_beams, "sub", 0, 0, tiled=True)
    return merge(near, image, from_far(image), tables)


def solution(mesh):
    split = Mesh(
        mesh.devices.reshape(mesh.shape["sub"], 2, RING, mesh.shape["comp"]), SUB_BEAM_COMP
    )
    return jax.shard_map(
        body,
        mesh=split,
        in_specs=(
            P(SUB_BEAM_COMP, None, None),
            P(),
            P(None, SUB_BEAM_COMP),
            P(None, BEAM_COMP),
            P(None, BEAM_COMP, None),
            P(None, BEAM_COMP),
        ),
        out_specs=P(BEAM_COMP, None, "sub"),
        check_vma=False,
    )
```

```python
import functools
import math

import jax
import jax.numpy as jnp
import ml_dtypes
import numpy as np
from jax import lax
from jax.experimental import pallas as pl
from jax.experimental.pallas import tpu as pltpu
from jax.sharding import Mesh
from jax.sharding import PartitionSpec as P

NR = 16384
RADIX = 128
NB0 = 8
BAND = 8
PSUB = 2048
RING = 4
WIDTHS = (8192, 8192)
READS = 8
READ = NR // READS
STEP = 2048
SLAB = NR // 8
COLS = 512
FIELDS = 256
CARRIED = 128
SIDE = 144
BEAM_COMP = ("y_hi", "z", "y_lo")
SUB_BEAM_COMP = ("sub", "y_hi", "z", "y_lo")
Y = ("y_hi", "y_lo")
Z = "z"
BF = jnp.bfloat16
F4 = jnp.float32
SENT = ((2, 0), (2, 1), (1, 2), (1, 3), (2, 2), (2, 3), (3, 0), (3, 1))
KEPT = ((1, 0), (1, 1), (3, 2), (3, 3), (0, 0), (0, 1), (0, 2), (0, 3))
KEPT_ROWS = (32, 32, 64)


def params(mebibytes):
    return pltpu.CompilerParams(vmem_limit_bytes=mebibytes << 20)


def real_form_transposed():
    index = np.arange(RADIX)
    angle = (index[:, None] * index[None, :] % RADIX) * (2.0 * math.pi / RADIX)
    cos_part, sin_part = np.cos(angle), -np.sin(angle)
    upper = np.concatenate([cos_part, sin_part], 1)
    lower = np.concatenate([-sin_part, cos_part], 1)
    return np.concatenate([upper, lower], 0).T.astype(ml_dtypes.bfloat16)


def twiddle():
    index = np.arange(RADIX)
    angle = (index[:, None] * index[None, :] % NR) * (2.0 * math.pi / NR)
    return np.stack([np.cos(angle), -np.sin(angle)]).astype(np.float32)


def ring_send(x, axis, step):
    return lax.ppermute(x, axis, [(k, (k + step) % RING) for k in range(RING)])


def steering_rows(angle_ref, weights):
    factor = float(PSUB) ** -0.5
    rows = lax.broadcasted_iota(jnp.int32, (128, 256), 0)
    cols = lax.broadcasted_iota(jnp.int32, (128, 256), 1)
    spread = jnp.where(cols // 2 == rows, 1.0, 0.0).astype(BF)
    angle = angle_ref[...]
    cosine = (jnp.cos(angle) * factor).astype(BF)
    sine = (jnp.sin(angle) * factor).astype(BF)
    cosine = jnp.dot(cosine, spread, preferred_element_type=F4)
    sine = jnp.dot(sine, spread, preferred_element_type=F4)
    even = cols % 2 == 0
    weights[0] = jnp.where(even, cosine, -sine)
    weights[1] = jnp.where(even, sine, cosine)


def beam_matrix(weights, owners, z_first):
    y = lax.axis_index("y_hi") * 2 + lax.axis_index("y_lo")
    z = lax.axis_index("z")
    picked = []
    for first, second in owners:
        y_step, z_step = (second, first) if z_first else (first, second)
        y_of, z_of = lax.rem(y + y_step, RING), lax.rem(z + z_step, RING)
        block = lax.div(y_of, 2) * 8 + z_of * 2 + lax.rem(y_of, 2)
        start = pl.multiple_of(block * NB0, NB0)
        picked.append(weights[0, pl.ds(start, NB0), :])
        picked.append(weights[1, pl.ds(start, NB0), :])
    return jnp.concatenate(picked, 0).astype(BF)


def spans(read):
    parts = []
    place = read * READ
    while place < (read + 1) * READ:
        half = int(place >= WIDTHS[0])
        limit = min((read + 1) * READ, place + STEP)
        if half == 0:
            limit = min(limit, WIDTHS[0])
        parts.append((half, place - read * READ, place - half * WIDTHS[0], limit - place))
        place = limit
    return parts


def split_three(table):
    parts = []
    for _ in range(3):
        part = table.astype(BF)
        parts.append(part)
        table = table - part.astype(F4)
    return parts


def carried_tables(parts):
    even = lax.axis_index("y_lo") == 0
    row = lax.broadcasted_iota(jnp.int32, (FIELDS, CARRIED), 0)
    lane = lax.broadcasted_iota(jnp.int32, (FIELDS, CARRIED), 1)
    side, k = lane % 32 // 16, lane % 16
    last = side * 128 + jnp.where(k < 8, k + 8, k + 32)
    first = side * 128 + jnp.where(k < 8, k, k + 8)
    rows = []
    for source in (jnp.where(even, last, first), jnp.where(even, first, last)):
        total = jnp.zeros((16, CARRIED), F4)
        for term, part in enumerate(parts):
            pick = jnp.where((row == source) & (lane // 32 == term), 1.0, 0.0).astype(BF)
            total = total + jnp.dot(part, pick, preferred_element_type=F4)
        rows.append(total)
    return jnp.concatenate([*rows, jnp.zeros((32, CARRIED), F4)], 0).astype(BF)


def opening_kernel(angle_ref, offset_ref, band_ref, delay_ref, raw_ref, *refs):
    outs, (weights, table) = refs[:4], refs[4:6]
    landed, angle_landed, offset_landed, band_landed, delay_landed, sems = refs[6:]
    small = (
        (angle_ref, angle_landed),
        (offset_ref, offset_landed),
        (band_ref, band_landed),
        (delay_ref, delay_landed),
    )
    small_reads = [
        pltpu.make_async_copy(source, target, sems.at[READS + k])
        for k, (source, target) in enumerate(small)
    ]
    for copy in small_reads:
        copy.start()

    def read(k):
        cols = pl.ds(k * READ, READ)
        return pltpu.make_async_copy(raw_ref.at[:, :, cols], landed.at[k], sems.at[k])

    for k in range(READS):
        read(k).start()
    for copy in small_reads:
        copy.wait()
    steering_rows(angle_landed, weights)
    width = offset_landed.shape[1]
    table[...] = jnp.zeros_like(table)
    for side in range(2):
        cols = slice(side * 128, side * 128 + width)
        table[0:1, cols] = offset_landed[side : side + 1, :].astype(F4)
        table[1:9, cols] = band_landed[side]
        table[9:10, cols] = delay_landed[side : side + 1, :]
    packed = carried_tables(split_three(table[...]))
    for out in outs[2:]:
        out[:, WIDTHS[1] :] = packed
    matrices = [beam_matrix(weights, SENT, half == 0) for half in range(2)]
    for k in range(READS):
        read(k).wait()
        for half, source, target, size in spans(k):
            raw = landed[k, :, :, source : source + size].reshape(256, size)
            total = jnp.dot(matrices[half], raw, preferred_element_type=F4).astype(BF)
            outs[2 * half][:, target : target + size] = total[:64]
            outs[2 * half + 1][:, target : target + size] = total[64:]


def opening_sums(raw, *small):
    vmem = pl.BlockSpec(memory_space=pltpu.VMEM)
    outs = [jax.ShapeDtypeStruct((64, c), BF) for c in (WIDTHS[0],) * 2 + (WIDTHS[1] + CARRIED,) * 2]
    outs += [jax.ShapeDtypeStruct((2, 128, 256), F4), jax.ShapeDtypeStruct((16, FIELDS), F4)]
    results = pl.pallas_call(
        opening_kernel,
        in_specs=[pl.BlockSpec(memory_space=pltpu.HBM)] * 5,
        out_specs=[vmem] * 6,
        out_shape=outs,
        scratch_shapes=[pltpu.VMEM((READS, 128, 2, READ), BF)]
        + [pltpu.VMEM(array.shape, array.dtype) for array in small]
        + [pltpu.SemaphoreType.DMA((READS + 4,))],
        compiler_params=params(20),
        name="opening_sums",
    )(*(pltpu.with_memory_space_constraint(a, pltpu.HBM) for a in (*small, raw)))
    return results[:2], results[2:4], *results[4:]


def later_kernel(weights, raw_ref, *outs):
    for k in range(READS):

        @pl.when(pl.program_id(0) == k)
        def _():
            for half, source, target, width in spans(k):
                matrix = beam_matrix(weights, KEPT, half == 0)
                raw = raw_ref[:, :, source : source + width].reshape(256, width)
                total = jnp.dot(matrix, raw, preferred_element_type=F4).astype(BF)
                start = 0
                for out in outs[3 * half : 3 * half + 3]:
                    size = out.shape[0]
                    out[:, target : target + width] = total[start : start + size]
                    start += size


def later_sums(weights, raw):
    vmem = pl.BlockSpec(memory_space=pltpu.VMEM)
    outs = [jax.ShapeDtypeStruct((n, c), BF) for c in WIDTHS for n in KEPT_ROWS]
    kept = pl.pallas_call(
        later_kernel,
        grid=(READS,),
        in_specs=[vmem, pl.BlockSpec((128, 2, READ), lambda i: (0, 0, i))],
        out_specs=[vmem] * 6,
        out_shape=outs,
        compiler_params=params(20),
        name="later_sums",
    )(weights, pltpu.with_memory_space_constraint(raw, pltpu.HBM))
    return kept[:3], kept[3:]


def relay(q, received):
    rows, cols = q.shape
    return (q.astype(F4) + received[:rows, :cols].astype(F4)).astype(BF)


def middle_kernel(own, p1, m1, p2, m2, plus, minus, q1, q3, keep):
    tile = 512

    def step(k, carry):
        cols = pl.ds(pl.multiple_of(k * tile, tile), tile)
        low = own[:32, cols].astype(F4) + m1[32:, cols].astype(F4) + p2[:, cols].astype(F4)
        high = own[32:, cols].astype(F4) + p1[32:, cols].astype(F4) + m2[:, cols].astype(F4)
        keep[:, cols] = low[:16]
        q1[:, cols] = low[16:24].astype(BF)
        plus[:, cols] = jnp.concatenate([high[:8], low[24:]], 0).astype(BF)
        minus[:, cols] = jnp.concatenate([high[8:16], high[16:24]], 0).astype(BF)
        q3[:, cols] = high[24:].astype(BF)
        return carry

    width = own.shape[1]
    lax.fori_loop(0, width // tile, step, 0)
    if plus.shape[1] > width:
        for j, received in enumerate((p1, m1)):
            cols = slice(width + j * CARRIED, width + (j + 1) * CARRIED)
            plus[:, cols] = received[16:32, width:]
            minus[:, cols] = received[16:32, width:]


def middle_sums(own, p1, m1, p2, m2):
    width = own.shape[1]
    wide = width + 2 * (p1.shape[1] - width)
    outs = ((16, wide, BF), (16, wide, BF), (8, width, BF), (8, width, BF), (16, width, F4))
    vmem = pl.BlockSpec(memory_space=pltpu.VMEM)
    return pl.pallas_call(
        middle_kernel,
        in_specs=[vmem] * 5,
        out_specs=[vmem] * 5,
        out_shape=[jax.ShapeDtypeStruct((n, c), d) for n, c, d in outs],
        compiler_params=params(4),
        name="middle_sums",
    )(own, p1, m1, p2, m2)


def compress_kernel(*refs):
    ins, (form_ref, turn_ref, filter_ref, out, lines, bins) = refs[:10], refs[10:]
    for half, width in enumerate(WIDTHS):
        keep, p3, m3, p4, m4 = ins[5 * half : 5 * half + 5]
        sums = (
            keep[:8] + m3[:, :width].astype(F4)[8:] + p4[...].astype(F4),
            keep[8:] + p3[:, :width].astype(F4)[8:] + m4[...].astype(F4),
        )
        for part in range(2):
            for k in range(width // 128):
                row = half * WIDTHS[0] // 16 + k * 8
                lines[part, row : row + 8, :] = sums[part][:, k * 128 : (k + 1) * 128]
    form = form_ref[...]
    cos_part, sin_part = turn_ref[0], turn_ref[1]
    scale = NR ** (-0.5)
    real_filter, imag_filter = filter_ref[0] * scale, filter_ref[1] * scale
    for beam in range(NB0):
        picked = pl.ds(beam, 128, stride=8)
        data = jnp.concatenate([lines[0, picked, :], lines[1, picked, :]], 0)
        upper = data.astype(BF)
        lower = (data - upper.astype(F4)).astype(BF)
        one = jnp.dot(form, jnp.concatenate([upper, lower], 1), preferred_element_type=F4)
        one = one[:, :128] + one[:, 128:]
        real_in, imag_in = one[:128], one[128:]
        turned = jnp.concatenate(
            [real_in * cos_part - imag_in * sin_part, real_in * sin_part + imag_in * cos_part], 1
        )
        upper = turned.astype(BF)
        lower = (turned - upper.astype(F4)).astype(BF)
        two = lax.dot_general(
            form,
            jnp.concatenate([upper, lower], 0),
            (((1,), (1,)), ((), ())),
            preferred_element_type=F4,
        )
        two = two[:, :128] + two[:, 128:]
        real_in, imag_in = two[:128], two[128:]
        bins[0, picked, :] = real_in * real_filter - imag_in * imag_filter
        bins[1, picked, :] = real_in * imag_filter + imag_in * real_filter
    for slab in range(8):
        for k in range(16):
            row = (slab * 16 + k) * 8
            both = jnp.concatenate([bins[0, row : row + 8, :], bins[1, row : row + 8, :]], 0)
            out[slab, :, k * 128 : (k + 1) * 128] = both.astype(BF)


def compressed_beams(pieces, range_filter):
    return pl.pallas_call(
        compress_kernel,
        out_shape=jax.ShapeDtypeStruct((8, 16, SLAB), BF),
        scratch_shapes=[pltpu.VMEM((2, 1024, 128), F4), pltpu.VMEM((2, 1024, 128), F4)],
        compiler_params=params(12),
        name="compressed_beams",
    )(
        *pieces,
        jnp.asarray(real_form_transposed()),
        jnp.asarray(twiddle()),
        range_filter.reshape(2, 128, 128),
    )


def sided(near, far):
    even = lax.axis_index("y_lo") == 0
    return jnp.where(even, far, near), jnp.where(even, near, far)


def table_kernel(start_ref, own_ref, y_below, y_above, z_below, z_above, *refs):
    first_matrix, matrix, near_cos, near_sin, far_cos, far_sin, lines = refs
    y_hi, z = lax.axis_index("y_hi"), lax.axis_index("z")
    even = lax.axis_index("y_lo") == 0

    def columns(fields):
        padded = jnp.concatenate([fields, jnp.zeros((112, 256), F4)], 0)
        return jnp.concatenate([padded[:, :128].T, padded[:, 128:].T], 0)

    def joined(parts):
        parts = parts.astype(F4)
        total = parts[:, :32] + parts[:, 32:64] + parts[:, 64:96]
        total = jnp.concatenate([total, jnp.zeros((16, 96), F4)], 1)
        return jnp.concatenate([total, jnp.zeros((112, 128), F4)], 0).T

    def from_rows(ref):
        return joined(ref[:16, WIDTHS[1] :])

    def from_cols(ref, j):
        first = WIDTHS[1] + j * CARRIED
        return joined(ref[:, first : first + CARRIED])

    near = jnp.where(even, from_rows(y_above), from_rows(y_below))
    left = jnp.where(z > 0, from_cols(z_below, 1), from_cols(z_below, 0))
    right = jnp.where(z < RING - 1, from_cols(z_above, 0), from_cols(z_above, 1))
    left = jnp.where((z > 0) | (y_hi > 0), left, 0.0)
    right = jnp.where((z < RING - 1) | (y_hi == 0), right, 0.0)
    left, right = sided(near, jnp.where(even, left, right))
    own = columns(own_ref[...])

    def piece(source, side, first, count, shift):
        start = side * (128 if source is own else 16) + first
        rows = source[start : start + count]
        field = lax.broadcasted_iota(jnp.int32, rows.shape, 1)
        return rows + jnp.where(field == 0, float(shift), 0.0)

    for side in range(2):
        row = side * SIDE
        for source, first, count, shift in (
            (left, 0, 8, 0),
            (own, 0, 16, 8),
            (right, 0, 8, 16),
            (left, 8, 8, -8),
            (own, 16, 32, 8),
            (right, 8, 8, 24),
            (own, 48, 64, 8),
        ):
            lines[row : row + count, :] = piece(source, side, first, count, shift)
            row += count
    rows = 2 * SIDE
    table = lines[...]
    lane = lax.broadcasted_iota(jnp.int32, (rows, 256), 1)
    row = lax.broadcasted_iota(jnp.int32, (rows, 256), 0) % SIDE
    depth = jnp.where(row < 80, 32, 48)
    term = lane // depth
    place = (lane - term * depth).astype(F4) - table[:, 0:1]
    band = jnp.zeros((rows, 256), F4)
    for tap in range(BAND):
        band = band + jnp.where(place == float(tap), table[:, tap + 1 : tap + 2], 0.0)
    upper = band.astype(BF).astype(F4)
    matrix[...] = jnp.where(term == 1, band - upper, upper).astype(BF)
    lane = lax.broadcasted_iota(jnp.int32, (32, 128), 1)
    term, inner = lane // 48, lane % 48
    block = jnp.where(even, 2 - inner // 16, inner // 16)
    child = (block * 8 + inner % 8).astype(F4)
    for side in range(2):
        fields = lines[side * SIDE : side * SIDE + 32, :]
        band = jnp.zeros((32, 128), F4)
        for tap in range(BAND):
            hit = child - fields[:, 0:1] == float(tap)
            band = band + jnp.where(hit, fields[:, tap + 1 : tap + 2], 0.0)
        upper = band.astype(BF).astype(F4)
        band = jnp.where(term == 1, band - upper, upper)
        for part in range(2):
            row = side * 64 + part * 32
            own_part = inner // 8 % 2 == part
            first_matrix[row : row + 32, :] = jnp.where(own_part, band, 0.0).astype(BF)
    delay = table[:, 9:10]
    lane = lax.broadcasted_iota(jnp.int32, (rows, 128), 1).astype(F4)
    step = delay * (lane * (1.0 / NR))
    far_cos[...] = jnp.cos(step)
    far_sin[...] = jnp.sin(step)
    first = start_ref[0].astype(F4)
    base = delay * (1.0 + (first + lane * 128.0) * (1.0 / NR))
    near_cos[...] = jnp.cos(base)
    near_sin[...] = jnp.sin(base)


def merge_tables(start, own, *received):
    rows = 2 * SIDE
    vmem = pl.BlockSpec(memory_space=pltpu.VMEM)
    return pl.pallas_call(
        table_kernel,
        grid=(1,),
        in_specs=[pl.BlockSpec(memory_space=pltpu.SMEM)] + [vmem] * 5,
        out_specs=[pl.BlockSpec((128, 128), lambda i: (0, 0))]
        + [pl.BlockSpec((rows, 256), lambda i: (0, 0))]
        + [pl.BlockSpec((rows, 128), lambda i: (0, 0))] * 4,
        out_shape=[pltpu.HBM((128, 128), BF), pltpu.HBM((rows, 256), BF)]
        + [pltpu.HBM((rows, 128), F4)] * 4,
        scratch_shapes=[pltpu.VMEM((rows, 128), F4)],
        compiler_params=params(12),
        name="merge_tables",
    )(start, own, *received)


def merge_kernel(near, own, far, first_matrix, matrix, *refs):
    near_cos, near_sin, far_cos, far_sin, out, lines = refs
    groups = COLS // 128
    place = pl.ds(pl.multiple_of(pl.program_id(0) * COLS, COLS), COLS)
    shift = lax.rem(128 - groups * pl.program_id(0), 128)
    cosines = pltpu.roll(near_cos[...], shift, 1)
    sines = pltpu.roll(near_sin[...], shift, 1)

    def phases(first, count):
        rows = slice(first, first + count)
        cosine, sine = far_cos[rows, :], far_sin[rows, :]
        real_parts, imag_parts = [], []
        for k in range(groups):
            a, b = cosines[rows, k : k + 1], sines[rows, k : k + 1]
            real_parts.append(a * cosine - b * sine)
            imag_parts.append(b * cosine + a * sine)
        return jnp.concatenate(real_parts, 1), jnp.concatenate(imag_parts, 1)

    def stacked(image):
        upper = image.astype(BF)
        lower = (image - upper.astype(F4)).astype(BF)
        return jnp.concatenate([upper, upper, lower], 0)

    def first_blend(side, sub):
        image = jnp.concatenate([ref[sub, :, place] for ref in (near, own, far)], 0)
        band = first_matrix[side * 64 : side * 64 + 64, :96]
        both = jnp.dot(band, jnp.concatenate([image, image], 0), preferred_element_type=F4)
        return both[:32], both[32:]

    images = range(8)
    for first, count, terms in ((0, 32, 0), (32, 48, 96), (80, 64, 144)):
        merged = [None] * (len(images) // 2)
        for side in range(2):
            start = side * SIDE + first
            cosine, sine = phases(start, count)
            for group in range(len(merged)):
                image = images[2 * group + side]
                if terms:
                    band = matrix[start : start + count, :terms]
                    real_in, imag_in = (
                        jnp.dot(band, stacked(part), preferred_element_type=F4) for part in image
                    )
                else:
                    real_in, imag_in = first_blend(side, image)
                real_out = cosine * real_in - sine * imag_in
                imag_out = sine * real_in + cosine * imag_in
                if side:
                    real_out, imag_out = merged[group][0] + real_out, merged[group][1] + imag_out
                merged[group] = (real_out, imag_out)
        images = merged
    for k in range(groups):
        cols = slice(k * 128, (k + 1) * 128)
        for part in range(2):
            lines[k, pl.ds(part, 64, stride=2), :] = images[0][part][:, cols]
        out[:, :, cols] = lines[k].reshape(64, 2, 128)


def merge(near, own, far, tables):
    rows = 2 * SIDE
    image = pl.BlockSpec(memory_space=pltpu.VMEM)
    whole = pl.BlockSpec((rows, 128), lambda i: (0, 0))
    return pl.pallas_call(
        merge_kernel,
        grid=(SLAB // COLS,),
        in_specs=[image] * 3
        + [pl.BlockSpec((128, 128), lambda i: (0, 0)), pl.BlockSpec((rows, 256), lambda i: (0, 0))]
        + [whole] * 4,
        out_specs=pl.BlockSpec((64, 2, COLS), lambda i: (0, 0, i)),
        out_shape=jax.ShapeDtypeStruct((64, 2, SLAB), F4),
        scratch_shapes=[pltpu.VMEM((COLS // 128, 128, 128), F4)],
        compiler_params=params(24),
        name="merge",
    )(near, own, far, *(pltpu.with_memory_space_constraint(t, pltpu.HBM) for t in tables))


def from_near(array):
    blocks = lax.axis_size(BEAM_COMP)
    return lax.ppermute(array, BEAM_COMP, [(k, k ^ 1) for k in range(blocks)])


def from_far(array):
    blocks = lax.axis_size(BEAM_COMP)
    steps = [(k, k - 1 + 2 * (k % 2)) for k in range(1, blocks - 1)]
    return lax.ppermute(array, BEAM_COMP, steps)


def ring_start(parts, first):
    return ring_send(parts[0], first, 1), ring_send(parts[1], first, -1)


def ring_rest(kept, received, first, second):
    q1, q3, own = kept
    p1, m1 = received
    p2 = ring_send(relay(q1, p1), first, 1)
    m2 = ring_send(relay(q3, m1), first, -1)
    plus, minus, q1, q3, keep = middle_sums(own, p1, m1, p2, m2)
    p3 = ring_send(plus, second, 1)
    m3 = ring_send(minus, second, -1)
    p4 = ring_send(relay(q1, p3), second, 1)
    m4 = ring_send(relay(q3, m3), second, -1)
    return keep, p3, m3, p4, m4


def body(raw_pulses, range_filter, steer_angle, band_offsets, band_weights, beam_delay):
    sent_z, sent_y, weights, table = opening_sums(
        raw_pulses, steer_angle, band_offsets, jnp.moveaxis(band_weights, 2, 1), beam_delay
    )
    received_z = ring_start(sent_z, Z)
    received_y = ring_start(sent_y, Y)
    kept_z, kept_y = later_sums(weights, raw_pulses)
    start = (lax.axis_index("sub") * SLAB).astype(jnp.int32).reshape(1)
    pieces_z = ring_rest(kept_z, received_z, Z, Y)
    pieces_y = ring_rest(kept_y, received_y, Y, Z)
    tables = merge_tables(start, table, *received_y, *pieces_y[1:3])
    beams = compressed_beams(pieces_z + pieces_y, range_filter)
    near_beams = from_near(beams)
    image = lax.all_to_all(beams, "sub", 0, 0, tiled=True)
    near = lax.all_to_all(near_beams, "sub", 0, 0, tiled=True)
    return merge(near, image, from_far(image), tables)


def solution(mesh):
    split = Mesh(
        mesh.devices.reshape(mesh.shape["sub"], 2, RING, mesh.shape["comp"]), SUB_BEAM_COMP
    )
    return jax.shard_map(
        body,
        mesh=split,
        in_specs=(
            P(SUB_BEAM_COMP, None, None),
            P(),
            P(None, SUB_BEAM_COMP),
            P(None, BEAM_COMP),
            P(None, BEAM_COMP, None),
            P(None, BEAM_COMP),
        ),
        out_specs=P(BEAM_COMP, None, "sub"),
        check_vma=False,
    )
```

```python
import functools
import math

import jax
import jax.numpy as jnp
import ml_dtypes
import numpy as np
from jax import lax
from jax.experimental import pallas as pl
from jax.experimental.pallas import tpu as pltpu
from jax.sharding import Mesh
from jax.sharding import PartitionSpec as P

NR = 16384
RADIX = 128
NB0 = 8
BAND = 8
PSUB = 2048
RING = 4
WIDTHS = (8192, 8192)
READS = 8
READ = NR // READS
STEP = 2048
SLAB = NR // 8
COLS = 1024
FIELDS = 256
CARRIED = 128
SIDE = 144
BEAM_COMP = ("y_hi", "z", "y_lo")
SUB_BEAM_COMP = ("sub", "y_hi", "z", "y_lo")
Y = ("y_hi", "y_lo")
Z = "z"
BF = jnp.bfloat16
F4 = jnp.float32
SENT = ((2, 0), (2, 1), (1, 2), (1, 3), (2, 2), (2, 3), (3, 0), (3, 1))
KEPT = ((1, 0), (1, 1), (3, 2), (3, 3), (0, 0), (0, 1), (0, 2), (0, 3))
KEPT_ROWS = (32, 32, 64)


def params(mebibytes):
    return pltpu.CompilerParams(vmem_limit_bytes=mebibytes << 20)


def real_form_transposed():
    index = np.arange(RADIX)
    angle = (index[:, None] * index[None, :] % RADIX) * (2.0 * math.pi / RADIX)
    cos_part, sin_part = np.cos(angle), -np.sin(angle)
    upper = np.concatenate([cos_part, sin_part], 1)
    lower = np.concatenate([-sin_part, cos_part], 1)
    return np.concatenate([upper, lower], 0).T.astype(ml_dtypes.bfloat16)


def twiddle():
    index = np.arange(RADIX)
    angle = (index[:, None] * index[None, :] % NR) * (2.0 * math.pi / NR)
    return np.stack([np.cos(angle), -np.sin(angle)]).astype(np.float32)


def ring_send(x, axis, step):
    return lax.ppermute(x, axis, [(k, (k + step) % RING) for k in range(RING)])


def steering_rows(angle_ref, weights):
    factor = float(PSUB) ** -0.5
    rows = lax.broadcasted_iota(jnp.int32, (128, 256), 0)
    cols = lax.broadcasted_iota(jnp.int32, (128, 256), 1)
    spread = jnp.where(cols // 2 == rows, 1.0, 0.0).astype(BF)
    angle = angle_ref[...]
    cosine = (jnp.cos(angle) * factor).astype(BF)
    sine = (jnp.sin(angle) * factor).astype(BF)
    cosine = jnp.dot(cosine, spread, preferred_element_type=F4)
    sine = jnp.dot(sine, spread, preferred_element_type=F4)
    even = cols % 2 == 0
    weights[0] = jnp.where(even, cosine, -sine)
    weights[1] = jnp.where(even, sine, cosine)


def beam_matrix(weights, owners, z_first):
    y = lax.axis_index("y_hi") * 2 + lax.axis_index("y_lo")
    z = lax.axis_index("z")
    picked = []
    for first, second in owners:
        y_step, z_step = (second, first) if z_first else (first, second)
        y_of, z_of = lax.rem(y + y_step, RING), lax.rem(z + z_step, RING)
        block = lax.div(y_of, 2) * 8 + z_of * 2 + lax.rem(y_of, 2)
        start = pl.multiple_of(block * NB0, NB0)
        picked.append(weights[0, pl.ds(start, NB0), :])
        picked.append(weights[1, pl.ds(start, NB0), :])
    return jnp.concatenate(picked, 0).astype(BF)


def spans(read):
    parts = []
    place = read * READ
    while place < (read + 1) * READ:
        half = int(place >= WIDTHS[0])
        limit = min((read + 1) * READ, place + STEP)
        if half == 0:
            limit = min(limit, WIDTHS[0])
        parts.append((half, place - read * READ, place - half * WIDTHS[0], limit - place))
        place = limit
    return parts


def split_three(table):
    parts = []
    for _ in range(3):
        part = table.astype(BF)
        parts.append(part)
        table = table - part.astype(F4)
    return parts


def carried_tables(parts):
    even = lax.axis_index("y_lo") == 0
    row = lax.broadcasted_iota(jnp.int32, (FIELDS, CARRIED), 0)
    lane = lax.broadcasted_iota(jnp.int32, (FIELDS, CARRIED), 1)
    side, k = lane % 32 // 16, lane % 16
    last = side * 128 + jnp.where(k < 8, k + 8, k + 32)
    first = side * 128 + jnp.where(k < 8, k, k + 8)
    rows = []
    for source in (jnp.where(even, last, first), jnp.where(even, first, last)):
        total = jnp.zeros((16, CARRIED), F4)
        for term, part in enumerate(parts):
            pick = jnp.where((row == source) & (lane // 32 == term), 1.0, 0.0).astype(BF)
            total = total + jnp.dot(part, pick, preferred_element_type=F4)
        rows.append(total)
    return jnp.concatenate([*rows, jnp.zeros((32, CARRIED), F4)], 0).astype(BF)


def opening_kernel(angle_ref, offset_ref, band_ref, delay_ref, raw_ref, *refs):
    outs, (weights, table) = refs[:4], refs[4:6]
    landed, angle_landed, offset_landed, band_landed, delay_landed, sems = refs[6:]
    small = (
        (angle_ref, angle_landed),
        (offset_ref, offset_landed),
        (band_ref, band_landed),
        (delay_ref, delay_landed),
    )
    small_reads = [
        pltpu.make_async_copy(source, target, sems.at[READS + k])
        for k, (source, target) in enumerate(small)
    ]
    for copy in small_reads:
        copy.start()

    def read(k):
        cols = pl.ds(k * READ, READ)
        return pltpu.make_async_copy(raw_ref.at[:, :, cols], landed.at[k], sems.at[k])

    for k in range(READS):
        read(k).start()
    for copy in small_reads:
        copy.wait()
    steering_rows(angle_landed, weights)
    width = offset_landed.shape[1]
    table[...] = jnp.zeros_like(table)
    for side in range(2):
        cols = slice(side * 128, side * 128 + width)
        table[0:1, cols] = offset_landed[side : side + 1, :].astype(F4)
        table[1:9, cols] = band_landed[side]
        table[9:10, cols] = delay_landed[side : side + 1, :]
    packed = carried_tables(split_three(table[...]))
    for out in outs[2:]:
        out[:, WIDTHS[1] :] = packed
    matrices = [beam_matrix(weights, SENT, half == 0) for half in range(2)]
    for k in range(READS):
        read(k).wait()
        for half, source, target, size in spans(k):
            raw = landed[k, :, :, source : source + size].reshape(256, size)
            total = jnp.dot(matrices[half], raw, preferred_element_type=F4).astype(BF)
            outs[2 * half][:, target : target + size] = total[:64]
            outs[2 * half + 1][:, target : target + size] = total[64:]


def opening_sums(raw, *small):
    vmem = pl.BlockSpec(memory_space=pltpu.VMEM)
    outs = [jax.ShapeDtypeStruct((64, c), BF) for c in (WIDTHS[0],) * 2 + (WIDTHS[1] + CARRIED,) * 2]
    outs += [jax.ShapeDtypeStruct((2, 128, 256), F4), jax.ShapeDtypeStruct((16, FIELDS), F4)]
    results = pl.pallas_call(
        opening_kernel,
        in_specs=[pl.BlockSpec(memory_space=pltpu.HBM)] * 5,
        out_specs=[vmem] * 6,
        out_shape=outs,
        scratch_shapes=[pltpu.VMEM((READS, 128, 2, READ), BF)]
        + [pltpu.VMEM(array.shape, array.dtype) for array in small]
        + [pltpu.SemaphoreType.DMA((READS + 4,))],
        compiler_params=params(20),
        name="opening_sums",
    )(*(pltpu.with_memory_space_constraint(a, pltpu.HBM) for a in (*small, raw)))
    return results[:2], results[2:4], *results[4:]


def later_kernel(weights, raw_ref, *outs):
    for k in range(READS):

        @pl.when(pl.program_id(0) == k)
        def _():
            for half, source, target, width in spans(k):
                matrix = beam_matrix(weights, KEPT, half == 0)
                raw = raw_ref[:, :, source : source + width].reshape(256, width)
                total = jnp.dot(matrix, raw, preferred_element_type=F4).astype(BF)
                start = 0
                for out in outs[3 * half : 3 * half + 3]:
                    size = out.shape[0]
                    out[:, target : target + width] = total[start : start + size]
                    start += size


def later_sums(weights, raw):
    vmem = pl.BlockSpec(memory_space=pltpu.VMEM)
    outs = [jax.ShapeDtypeStruct((n, c), BF) for c in WIDTHS for n in KEPT_ROWS]
    kept = pl.pallas_call(
        later_kernel,
        grid=(READS,),
        in_specs=[vmem, pl.BlockSpec((128, 2, READ), lambda i: (0, 0, i))],
        out_specs=[vmem] * 6,
        out_shape=outs,
        compiler_params=params(20),
        name="later_sums",
    )(weights, pltpu.with_memory_space_constraint(raw, pltpu.HBM))
    return kept[:3], kept[3:]


def relay(q, received):
    rows, cols = q.shape
    return (q.astype(F4) + received[:rows, :cols].astype(F4)).astype(BF)


def middle_kernel(own, p1, m1, p2, m2, plus, minus, q1, q3, keep):
    tile = 1024

    def step(k, carry):
        cols = pl.ds(pl.multiple_of(k * tile, tile), tile)
        low = own[:32, cols].astype(F4) + m1[32:, cols].astype(F4) + p2[:, cols].astype(F4)
        high = own[32:, cols].astype(F4) + p1[32:, cols].astype(F4) + m2[:, cols].astype(F4)
        keep[:, cols] = low[:16]
        q1[:, cols] = low[16:24].astype(BF)
        plus[:, cols] = jnp.concatenate([high[:8], low[24:]], 0).astype(BF)
        minus[:, cols] = jnp.concatenate([high[8:16], high[16:24]], 0).astype(BF)
        q3[:, cols] = high[24:].astype(BF)
        return carry

    width = own.shape[1]
    lax.fori_loop(0, width // tile, step, 0)
    if plus.shape[1] > width:
        for j, received in enumerate((p1, m1)):
            cols = slice(width + j * CARRIED, width + (j + 1) * CARRIED)
            plus[:, cols] = received[16:32, width:]
            minus[:, cols] = received[16:32, width:]


def middle_sums(own, p1, m1, p2, m2):
    width = own.shape[1]
    wide = width + 2 * (p1.shape[1] - width)
    outs = ((16, wide, BF), (16, wide, BF), (8, width, BF), (8, width, BF), (16, width, F4))
    vmem = pl.BlockSpec(memory_space=pltpu.VMEM)
    return pl.pallas_call(
        middle_kernel,
        in_specs=[vmem] * 5,
        out_specs=[vmem] * 5,
        out_shape=[jax.ShapeDtypeStruct((n, c), d) for n, c, d in outs],
        compiler_params=params(4),
        name="middle_sums",
    )(own, p1, m1, p2, m2)


def compress_kernel(*refs):
    ins, (form_ref, turn_ref, filter_ref, out, lines, bins) = refs[:10], refs[10:]
    for half, width in enumerate(WIDTHS):
        keep, p3, m3, p4, m4 = ins[5 * half : 5 * half + 5]
        sums = (
            keep[:8] + m3[:, :width].astype(F4)[8:] + p4[...].astype(F4),
            keep[8:] + p3[:, :width].astype(F4)[8:] + m4[...].astype(F4),
        )
        for part in range(2):
            for k in range(width // 128):
                row = half * WIDTHS[0] // 16 + k * 8
                lines[part, row : row + 8, :] = sums[part][:, k * 128 : (k + 1) * 128]
    form = form_ref[...]
    cos_part, sin_part = turn_ref[0], turn_ref[1]
    scale = NR ** (-0.5)
    real_filter, imag_filter = filter_ref[0] * scale, filter_ref[1] * scale
    for beam in range(NB0):
        picked = pl.ds(beam, 128, stride=8)
        data = jnp.concatenate([lines[0, picked, :], lines[1, picked, :]], 0)
        upper = data.astype(BF)
        lower = (data - upper.astype(F4)).astype(BF)
        one = jnp.dot(form, jnp.concatenate([upper, lower], 1), preferred_element_type=F4)
        one = one[:, :128] + one[:, 128:]
        real_in, imag_in = one[:128], one[128:]
        turned = jnp.concatenate(
            [real_in * cos_part - imag_in * sin_part, real_in * sin_part + imag_in * cos_part], 1
        )
        upper = turned.astype(BF)
        lower = (turned - upper.astype(F4)).astype(BF)
        two = lax.dot_general(
            form,
            jnp.concatenate([upper, lower], 0),
            (((1,), (1,)), ((), ())),
            preferred_element_type=F4,
        )
        two = two[:, :128] + two[:, 128:]
        real_in, imag_in = two[:128], two[128:]
        bins[0, picked, :] = real_in * real_filter - imag_in * imag_filter
        bins[1, picked, :] = real_in * imag_filter + imag_in * real_filter
    for slab in range(8):
        for k in range(16):
            row = (slab * 16 + k) * 8
            both = jnp.concatenate([bins[0, row : row + 8, :], bins[1, row : row + 8, :]], 0)
            out[slab, :, k * 128 : (k + 1) * 128] = both.astype(BF)


def compressed_beams(pieces, range_filter):
    return pl.pallas_call(
        compress_kernel,
        out_shape=jax.ShapeDtypeStruct((8, 16, SLAB), BF),
        scratch_shapes=[pltpu.VMEM((2, 1024, 128), F4), pltpu.VMEM((2, 1024, 128), F4)],
        compiler_params=params(12),
        name="compressed_beams",
    )(
        *pieces,
        jnp.asarray(real_form_transposed()),
        jnp.asarray(twiddle()),
        range_filter.reshape(2, 128, 128),
    )


def sided(near, far):
    even = lax.axis_index("y_lo") == 0
    return jnp.where(even, far, near), jnp.where(even, near, far)


def table_kernel(start_ref, own_ref, y_below, y_above, z_below, z_above, *refs):
    first_matrix, matrix, near_cos, near_sin, far_cos, far_sin, lines = refs
    y_hi, z = lax.axis_index("y_hi"), lax.axis_index("z")
    even = lax.axis_index("y_lo") == 0

    def columns(fields):
        padded = jnp.concatenate([fields, jnp.zeros((112, 256), F4)], 0)
        return jnp.concatenate([padded[:, :128].T, padded[:, 128:].T], 0)

    def joined(parts):
        parts = parts.astype(F4)
        total = parts[:, :32] + parts[:, 32:64] + parts[:, 64:96]
        total = jnp.concatenate([total, jnp.zeros((16, 96), F4)], 1)
        return jnp.concatenate([total, jnp.zeros((112, 128), F4)], 0).T

    def from_rows(ref):
        return joined(ref[:16, WIDTHS[1] :])

    def from_cols(ref, j):
        first = WIDTHS[1] + j * CARRIED
        return joined(ref[:, first : first + CARRIED])

    near = jnp.where(even, from_rows(y_above), from_rows(y_below))
    left = jnp.where(z > 0, from_cols(z_below, 1), from_cols(z_below, 0))
    right = jnp.where(z < RING - 1, from_cols(z_above, 0), from_cols(z_above, 1))
    left = jnp.where((z > 0) | (y_hi > 0), left, 0.0)
    right = jnp.where((z < RING - 1) | (y_hi == 0), right, 0.0)
    left, right = sided(near, jnp.where(even, left, right))
    own = columns(own_ref[...])

    def piece(source, side, first, count, shift):
        start = side * (128 if source is own else 16) + first
        rows = source[start : start + count]
        field = lax.broadcasted_iota(jnp.int32, rows.shape, 1)
        return rows + jnp.where(field == 0, float(shift), 0.0)

    for side in range(2):
        row = side * SIDE
        for source, first, count, shift in (
            (left, 0, 8, 0),
            (own, 0, 16, 8),
            (right, 0, 8, 16),
            (left, 8, 8, -8),
            (own, 16, 32, 8),
            (right, 8, 8, 24),
            (own, 48, 64, 8),
        ):
            lines[row : row + count, :] = piece(source, side, first, count, shift)
            row += count
    rows = 2 * SIDE
    table = lines[...]
    lane = lax.broadcasted_iota(jnp.int32, (rows, 256), 1)
    row = lax.broadcasted_iota(jnp.int32, (rows, 256), 0) % SIDE
    depth = jnp.where(row < 80, 32, 48)
    term = lane // depth
    place = (lane - term * depth).astype(F4) - table[:, 0:1]
    band = jnp.zeros((rows, 256), F4)
    for tap in range(BAND):
        band = band + jnp.where(place == float(tap), table[:, tap + 1 : tap + 2], 0.0)
    upper = band.astype(BF).astype(F4)
    matrix[...] = jnp.where(term == 1, band - upper, upper).astype(BF)
    lane = lax.broadcasted_iota(jnp.int32, (32, 128), 1)
    term, inner = lane // 48, lane % 48
    block = jnp.where(even, 2 - inner // 16, inner // 16)
    child = (block * 8 + inner % 8).astype(F4)
    for side in range(2):
        fields = lines[side * SIDE : side * SIDE + 32, :]
        band = jnp.zeros((32, 128), F4)
        for tap in range(BAND):
            hit = child - fields[:, 0:1] == float(tap)
            band = band + jnp.where(hit, fields[:, tap + 1 : tap + 2], 0.0)
        upper = band.astype(BF).astype(F4)
        band = jnp.where(term == 1, band - upper, upper)
        for part in range(2):
            row = side * 64 + part * 32
            own_part = inner // 8 % 2 == part
            first_matrix[row : row + 32, :] = jnp.where(own_part, band, 0.0).astype(BF)
    delay = table[:, 9:10]
    lane = lax.broadcasted_iota(jnp.int32, (rows, 128), 1).astype(F4)
    step = delay * (lane * (1.0 / NR))
    far_cos[...] = jnp.cos(step)
    far_sin[...] = jnp.sin(step)
    first = start_ref[0].astype(F4)
    base = delay * (1.0 + (first + lane * 128.0) * (1.0 / NR))
    near_cos[...] = jnp.cos(base)
    near_sin[...] = jnp.sin(base)


def merge_tables(start, own, *received):
    rows = 2 * SIDE
    vmem = pl.BlockSpec(memory_space=pltpu.VMEM)
    return pl.pallas_call(
        table_kernel,
        grid=(1,),
        in_specs=[pl.BlockSpec(memory_space=pltpu.SMEM)] + [vmem] * 5,
        out_specs=[pl.BlockSpec((128, 128), lambda i: (0, 0))]
        + [pl.BlockSpec((rows, 256), lambda i: (0, 0))]
        + [pl.BlockSpec((rows, 128), lambda i: (0, 0))] * 4,
        out_shape=[pltpu.HBM((128, 128), BF), pltpu.HBM((rows, 256), BF)]
        + [pltpu.HBM((rows, 128), F4)] * 4,
        scratch_shapes=[pltpu.VMEM((rows, 128), F4)],
        compiler_params=params(12),
        name="merge_tables",
    )(start, own, *received)


def merge_kernel(near, own, far, first_matrix, matrix, *refs):
    near_cos, near_sin, far_cos, far_sin, out, lines = refs
    groups = COLS // 128
    place = pl.ds(pl.multiple_of(pl.program_id(0) * COLS, COLS), COLS)
    shift = lax.rem(128 - groups * pl.program_id(0), 128)
    cosines = pltpu.roll(near_cos[...], shift, 1)
    sines = pltpu.roll(near_sin[...], shift, 1)

    def phases(first, count):
        rows = slice(first, first + count)
        cosine, sine = far_cos[rows, :], far_sin[rows, :]
        real_parts, imag_parts = [], []
        for k in range(groups):
            a, b = cosines[rows, k : k + 1], sines[rows, k : k + 1]
            real_parts.append(a * cosine - b * sine)
            imag_parts.append(b * cosine + a * sine)
        return jnp.concatenate(real_parts, 1), jnp.concatenate(imag_parts, 1)

    def stacked(image):
        upper = image.astype(BF)
        lower = (image - upper.astype(F4)).astype(BF)
        return jnp.concatenate([upper, upper, lower], 0)

    def first_blend(side, sub):
        image = jnp.concatenate([ref[sub, :, place] for ref in (near, own, far)], 0)
        band = first_matrix[side * 64 : side * 64 + 64, :96]
        both = jnp.dot(band, jnp.concatenate([image, image], 0), preferred_element_type=F4)
        return both[:32], both[32:]

    images = range(8)
    for first, count, terms in ((0, 32, 0), (32, 48, 96), (80, 64, 144)):
        merged = [None] * (len(images) // 2)
        for side in range(2):
            start = side * SIDE + first
            cosine, sine = phases(start, count)
            for group in range(len(merged)):
                image = images[2 * group + side]
                if terms:
                    band = matrix[start : start + count, :terms]
                    real_in, imag_in = (
                        jnp.dot(band, stacked(part), preferred_element_type=F4) for part in image
                    )
                else:
                    real_in, imag_in = first_blend(side, image)
                real_out = cosine * real_in - sine * imag_in
                imag_out = sine * real_in + cosine * imag_in
                if side:
                    real_out, imag_out = merged[group][0] + real_out, merged[group][1] + imag_out
                merged[group] = (real_out, imag_out)
        images = merged
    for k in range(groups):
        cols = slice(k * 128, (k + 1) * 128)
        for part in range(2):
            lines[k, pl.ds(part, 64, stride=2), :] = images[0][part][:, cols]
        out[:, :, cols] = lines[k].reshape(64, 2, 128)


def merge(near, own, far, tables):
    rows = 2 * SIDE
    image = pl.BlockSpec(memory_space=pltpu.VMEM)
    whole = pl.BlockSpec((rows, 128), lambda i: (0, 0))
    return pl.pallas_call(
        merge_kernel,
        grid=(SLAB // COLS,),
        in_specs=[image] * 3
        + [pl.BlockSpec((128, 128), lambda i: (0, 0)), pl.BlockSpec((rows, 256), lambda i: (0, 0))]
        + [whole] * 4,
        out_specs=pl.BlockSpec((64, 2, COLS), lambda i: (0, 0, i)),
        out_shape=jax.ShapeDtypeStruct((64, 2, SLAB), F4),
        scratch_shapes=[pltpu.VMEM((COLS // 128, 128, 128), F4)],
        compiler_params=params(24),
        name="merge",
    )(near, own, far, *(pltpu.with_memory_space_constraint(t, pltpu.HBM) for t in tables))


def from_near(array):
    blocks = lax.axis_size(BEAM_COMP)
    return lax.ppermute(array, BEAM_COMP, [(k, k ^ 1) for k in range(blocks)])


def from_far(array):
    blocks = lax.axis_size(BEAM_COMP)
    steps = [(k, k - 1 + 2 * (k % 2)) for k in range(1, blocks - 1)]
    return lax.ppermute(array, BEAM_COMP, steps)


def ring_start(parts, first):
    return ring_send(parts[0], first, 1), ring_send(parts[1], first, -1)


def ring_rest(kept, received, first, second):
    q1, q3, own = kept
    p1, m1 = received
    p2 = ring_send(relay(q1, p1), first, 1)
    m2 = ring_send(relay(q3, m1), first, -1)
    plus, minus, q1, q3, keep = middle_sums(own, p1, m1, p2, m2)
    p3 = ring_send(plus, second, 1)
    m3 = ring_send(minus, second, -1)
    p4 = ring_send(relay(q1, p3), second, 1)
    m4 = ring_send(relay(q3, m3), second, -1)
    return keep, p3, m3, p4, m4


def body(raw_pulses, range_filter, steer_angle, band_offsets, band_weights, beam_delay):
    sent_z, sent_y, weights, table = opening_sums(
        raw_pulses, steer_angle, band_offsets, jnp.moveaxis(band_weights, 2, 1), beam_delay
    )
    received_z = ring_start(sent_z, Z)
    received_y = ring_start(sent_y, Y)
    kept_z, kept_y = later_sums(weights, raw_pulses)
    start = (lax.axis_index("sub") * SLAB).astype(jnp.int32).reshape(1)
    pieces_z = ring_rest(kept_z, received_z, Z, Y)
    pieces_y = ring_rest(kept_y, received_y, Y, Z)
    tables = merge_tables(start, table, *received_y, *pieces_y[1:3])
    beams = compressed_beams(pieces_z + pieces_y, range_filter)
    near_beams = from_near(beams)
    image = lax.all_to_all(beams, "sub", 0, 0, tiled=True)
    near = lax.all_to_all(near_beams, "sub", 0, 0, tiled=True)
    return merge(near, image, from_far(image), tables)


def solution(mesh):
    split = Mesh(
        mesh.devices.reshape(mesh.shape["sub"], 2, RING, mesh.shape["comp"]), SUB_BEAM_COMP
    )
    return jax.shard_map(
        body,
        mesh=split,
        in_specs=(
            P(SUB_BEAM_COMP, None, None),
            P(),
            P(None, SUB_BEAM_COMP),
            P(None, BEAM_COMP),
            P(None, BEAM_COMP, None),
            P(None, BEAM_COMP),
        ),
        out_specs=P(BEAM_COMP, None, "sub"),
        check_vma=False,
    )
```
